128 devices in a mesh: expert: 16 (over y, z), dp: 8 (over x, core).
Axes of the slice: x: 4, y: 4, z: 4, core: 2. Of those that a mesh axis runs over, the one named last changes fastest.
Arguments:
- tokens: bfloat16 [32768, 2048], P(('expert', 'dp')), may hold values from -6 to 6
- out_grad: bfloat16 [32768, 2048], P(('expert', 'dp')), may hold values from -6 to 6
- weights: bfloat16 [16, 2048, 4224], P('expert'), may hold values from -0.125 to 0.125
- gate_values: float32 [16, 1024], P('expert', 'dp'), may hold values from 0.1 to 1
- expert_picks: int32 [16, 1024], replicated, may hold values from 0 to 32767, as said below
Outputs:
- token_grad: bfloat16 [32768, 2048], P(('expert', 'dp'))
- weight_grad: bfloat16 [16, 2048, 4224], P('expert', 'dp')
- gate_grad: float32 [16, 1024], P('expert', 'dp')
The draws below stay inside these ranges and needn't reach their ends.
Inputs may be any that keep to these rules, and one draw needn't show every extreme that they name: `expert_picks`: each expert's 1024 picks are distinct tokens. In each aligned block of 128 picks of one expert, at most 2 picks are among the 256 consecutive tokens of any one device, and exactly 2 for some device.
All inputs are finite; a program needn't handle non-finite values.
Results may differ from the reference program's by a relative error of at most 0.0058.
Values may be sent and summed in bfloat16 or wider, within the bound.
A program may use at most 192 MiB of HBM per device.

```python
import math
import jax
import jax.numpy as jnp
from jax import lax

D = 2048
H = 1408
TOK_DEV = 256
EXPERTS = 16
TOKENS = 32768
CAP = 1024
ROWS = 128
HOLDERS = 128
MEAN_PAIR = 1
SLOT = 2


def block_counts(ordering_key, shift_key):
    ordering = jax.random.permutation(ordering_key, HOLDERS)
    shifts = jax.random.randint(shift_key, (HOLDERS // 2,), -MEAN_PAIR, MEAN_PAIR + 1)
    shifts = shifts.at[0].set(MEAN_PAIR)
    counts = jnp.zeros((HOLDERS,), jnp.int32)
    counts = counts.at[ordering[0::2]].set(MEAN_PAIR + shifts)
    counts = counts.at[ordering[1::2]].set(MEAN_PAIR - shifts)
    return counts


def draw_expert_picks(key, part):
    blocks = CAP // ROWS
    split_keys = jax.random.split(key, 4)
    count_keys = jax.random.split(split_keys[0], EXPERTS * blocks)
    shift_keys = jax.random.split(split_keys[1], EXPERTS * blocks)
    counts = jax.vmap(block_counts)(count_keys, shift_keys).reshape(EXPERTS, blocks, HOLDERS)
    starts = jnp.cumsum(counts, axis=1) - counts
    token_keys = jax.random.split(split_keys[2], EXPERTS * HOLDERS)
    shuffled = jax.vmap(lambda subkey: jax.random.permutation(subkey, TOK_DEV))(token_keys)
    within = jnp.arange(SLOT, dtype=jnp.int32)[None, None, None, :]
    filled = within < counts[:, :, :, None]
    places = jnp.minimum(starts[:, :, :, None] + within, TOK_DEV - 1)
    expert_ids = jnp.arange(EXPERTS, dtype=jnp.int32)[:, None, None, None]
    holder_ids = jnp.arange(HOLDERS, dtype=jnp.int32)[None, None, :, None]
    local_rows = shuffled.reshape(-1)[(expert_ids * HOLDERS + holder_ids) * TOK_DEV + places]
    candidates = (holder_ids * TOK_DEV + local_rows).reshape(EXPERTS * blocks, HOLDERS * SLOT)
    filled = filled.reshape(EXPERTS * blocks, HOLDERS * SLOT)
    ordering_keys = jax.random.split(split_keys[3], EXPERTS * blocks)
    scores = jax.vmap(lambda subkey: jax.random.permutation(subkey, HOLDERS * SLOT))(ordering_keys)
    scores = jnp.where(filled, scores + HOLDERS * SLOT, scores)
    chosen = jnp.argsort(-scores, axis=1, stable=True)[:, :ROWS]
    picked = jnp.take_along_axis(candidates, chosen, axis=1)
    return picked.reshape(EXPERTS, CAP).astype(jnp.int32)


def steps_of(rng, extent, cuts, low, largest):
    factor_of = 1.0
    for axis_at, blocks in cuts:
        heights = jax.random.uniform(jax.random.fold_in(jax.random.fold_in(rng, 6), axis_at), (blocks,), jnp.float32, low / len(cuts), largest / len(cuts))
        factor_of = factor_of * jnp.repeat(jnp.exp(heights), extent[axis_at] // blocks).reshape((-1,) + (1,) * (len(extent) - 1 - axis_at))
    return factor_of


def normal_values(rng, extent, scale, most, cuts=(), kind=jnp.bfloat16):
    drawn = jax.random.normal(rng, extent, jnp.float32) * scale
    if len(cuts) > 0:
        drawn = steps_of(rng, extent, cuts, -0.22, 0.18) * drawn
    return jnp.clip(drawn, min=-most, max=most).astype(kind)


def setup_inputs(seed: int = 0) -> dict:
    splits = jax.random.split(jax.random.key(seed), 6)
    tokens = normal_values(splits[0], (TOKENS, D), 1.0, 6.0, ((0, 128),))
    out_grad = normal_values(splits[1], (TOKENS, D), 1.0, 6.0, ((0, 128),))
    weights = normal_values(splits[2], (EXPERTS, D, 3 * H), D ** -0.5, 0.125, ((0, 16),))
    gate_values = jnp.clip(jnp.exp(math.log(1.0) - 2.3025851 * jax.random.uniform(splits[3], (EXPERTS, CAP), jnp.float32) ** steps_of(splits[3], (EXPERTS, CAP), ((0, 16), (1, 8)), -0.2, 0.2)), 0.1, 1.0)
    expert_picks = draw_expert_picks(jax.random.fold_in(splits[5], 71), 0)
    return dict(tokens=tokens, out_grad=out_grad, weights=weights, gate_values=gate_values, expert_picks=expert_picks)


def expert_pass(inputs, upstream, scales, matrix):
    hidden_width = matrix.shape[1] // 3
    gate_up = matrix[:, :2 * hidden_width]
    down_proj = matrix[:, 2 * hidden_width:]
    projected = jnp.dot(inputs, gate_up, preferred_element_type=jnp.float32)
    gate_pre = projected[:, :hidden_width]
    up_values = projected[:, hidden_width:]
    logistic = jax.nn.sigmoid(gate_pre)
    activated = gate_pre * logistic
    hidden = (activated * up_values).astype(jnp.bfloat16)
    contract = (((1,), (1,)), ((), ()))
    output = lax.dot_general(hidden, down_proj, contract, preferred_element_type=jnp.float32)
    gate_grad = jnp.sum(upstream.astype(jnp.float32) * output, axis=1)
    scaled = (scales[:, None] * upstream.astype(jnp.float32)).astype(jnp.bfloat16)
    hidden_grad = jnp.dot(scaled, down_proj, preferred_element_type=jnp.float32)
    pre_grad = (hidden_grad * up_values * logistic * (1.0 + gate_pre * (1.0 - logistic))).astype(jnp.bfloat16)
    up_grad = (hidden_grad * activated).astype(jnp.bfloat16)
    joint_grad = jnp.concatenate([pre_grad, up_grad], axis=1)
    token_part = lax.dot_general(joint_grad, gate_up, contract, preferred_element_type=jnp.float32)
    return token_part, gate_grad, joint_grad, hidden, scaled


def reference(tokens, out_grad, weights, gate_values, expert_picks):
    contract_rows = (((0,), (0,)), ((), ()))

    def one_expert(summed, members):
        matrix, scales, chosen = members
        inputs = tokens[chosen]
        upstream = out_grad[chosen]
        token_part, gate_grad, joint_grad, hidden, scaled = expert_pass(inputs, upstream, scales, matrix)
        left_part = lax.dot_general(inputs, joint_grad, contract_rows, preferred_element_type=jnp.float32)
        right_part = lax.dot_general(scaled, hidden, contract_rows, preferred_element_type=jnp.float32)
        weight_grad = jnp.concatenate([left_part, right_part], axis=1).astype(jnp.bfloat16)
        summed = summed.at[chosen].add(token_part)
        return summed, (weight_grad, gate_grad)

    initial = jnp.zeros((TOKENS, D), jnp.float32)
    summed, stacked = lax.scan(one_expert, initial, (weights, gate_values, expert_picks))
    return summed.astype(jnp.bfloat16), stacked[0], stacked[1]
```

```python
import functools

import jax
import jax.numpy as jnp
from jax import lax
from jax.experimental import pallas as pl
from jax.experimental.pallas import tpu as pltpu
from jax.sharding import PartitionSpec as P

MESH = pl.DeviceIdType.MESH
F32 = jnp.float32
BF16 = jnp.bfloat16
I32 = jnp.int32
D = 2048
H = 1408
EXPERTS = 16
DP = 8
TOK = 256
SLOTS = 256
ROWS = 128
TILES = ((0, 256), (256, 256), (512, 256), (768, 256), (1024, 256), (1280, 128))


def iota(shape, axis):
    return lax.broadcasted_iota(I32, shape, axis)


def matmul(a, b):
    return jnp.dot(a, b, preferred_element_type=F32)


def matmul_tn(a, b):
    return lax.dot_general(a, b, (((0,), (0,)), ((), ())), preferred_element_type=F32)


def matmul_nt(a, b):
    return lax.dot_general(a, b, (((1,), (1,)), ((), ())), preferred_element_type=F32)


def slot_column(mask, values, tri):
    ones = jnp.where(mask, 1.0, 0.0)
    rank = matmul(ones.astype(BF16), tri) * ones
    rank3 = rank.reshape(16, 8, 128)
    value3 = values.reshape(16, 8, 128)
    ranks = jnp.concatenate([rank3, rank3], axis=1).reshape(SLOTS, 128)
    twice = jnp.concatenate([value3, value3], axis=1).reshape(SLOTS, 128)
    wanted = ((iota((SLOTS, 128), 0) // 8) % 2 + 1).astype(F32)
    return jnp.sum(jnp.where(ranks == wanted, twice + 1.0, 0.0), axis=1, keepdims=True) - 1.0


def kernel(
    cap,
    picks_ref,
    gates_ref,
    tok_ref,
    grad_ref,
    w_hbm,
    token_out,
    weight_out,
    gate_out,
    w,
    send,
    recv,
    gathered,
    joint,
    acc,
    back_send,
    back_recv,
    sel,
    pack,
    own_rows,
    place,
    all_gates,
    w_sem,
    s1_send,
    s1_recv,
    gate_send,
    gate_recv,
    ring_send,
    ring_recv,
    back_send_sem,
    back_recv_sem,
):
    e = lax.axis_index("expert")
    d = lax.axis_index("dp")
    ey, ez = e // 4, e % 4
    x, core = d // 2, d % 2
    me = e * DP + d
    right = ((x + 1) % 4) * 2 + core
    left = ((x + 3) % 4) * 2 + core
    other = x * 2 + 1 - core

    load_w = pltpu.make_async_copy(w_hbm, w, w_sem)
    load_w.start()

    def peer(k):
        return ((ey + k // 4) % 4) * 4 + (ez + k % 4) % 4

    def source(k):
        return ((ey + 4 - k // 4) % 4) * 4 + (ez + 4 - k % 4) % 4

    barrier = pltpu.get_barrier_semaphore()

    @pl.loop(1, 16)
    def _(k):
        pl.semaphore_signal(barrier, inc=1, device_id=(peer(k), d), device_id_type=MESH)

    @pl.loop(1, 8)
    def _(k):
        pl.semaphore_signal(barrier, inc=1, device_id=(e, (d + k) % 8), device_id_type=MESH)

    tri = jnp.where(iota((128, 128), 0) <= iota((128, 128), 1), 1.0, 0.0).astype(BF16)
    picks = picks_ref[...]
    token_of = slot_column((picks >> 8) == me, (picks & 255).astype(F32), tri)
    sel[...] = jnp.where(token_of == iota((SLOTS, TOK), 1).astype(F32), 1.0, 0.0).astype(BF16)
    all_gates[d] = jnp.broadcast_to(gates_ref[...], (8, 128))

    def block(ref, row):
        return ref.at[pl.ds(pl.multiple_of(row * 16, 16), 16), :]

    def s1_copy(h, k):
        return pltpu.make_async_remote_copy(
            src_ref=block(send.at[h], peer(k)),
            dst_ref=block(recv.at[h], e),
            send_sem=s1_send.at[h, k],
            recv_sem=s1_recv.at[h, k],
            device_id=(peer(k), d),
            device_id_type=MESH,
        )

    def gate_copy(k):
        return pltpu.make_async_remote_copy(
            src_ref=all_gates.at[d],
            dst_ref=all_gates.at[d],
            send_sem=gate_send.at[k],
            recv_sem=gate_recv.at[k],
            device_id=(e, (d + k) % 8),
            device_id_type=MESH,
        )

    for h, ref in ((0, tok_ref), (1, grad_ref)):
        send[h] = matmul(sel[...], ref[...]).astype(BF16)
        if h == 0:
            pl.semaphore_wait(barrier, 22)

        @pl.loop(1, 16)
        def _(k, h=h):
            s1_copy(h, k).start()

        own = pl.ds(pl.multiple_of(e * 16, 16), 16)
        recv[h, own, :] = send[h, own, :]

    @pl.loop(1, 8)
    def _(k):
        gate_copy(k).start()

    mine = picks_ref[pl.ds(pl.multiple_of(e * 8, 8), 8), :]
    sources = mine >> 8
    planes = sources & 7
    before = jnp.zeros((8, 1), F32)
    positions = []
    for b in range(8):
        hit = jnp.where(
            jnp.broadcast_to(planes[b : b + 1, :], (8, 128)) == iota((8, 128), 0), 1.0, 0.0
        )
        count = matmul(hit.astype(BF16), tri)
        positions.append(jnp.sum(hit * (count + before), axis=0, keepdims=True) - 1.0)
        before = before + count[:, 127:128]
    position = jnp.concatenate(positions, axis=0)
    rows_of = position + planes.astype(F32) * cap
    for b in range(8):
        place[:, b * 128 : (b + 1) * 128] = rows_of[b : b + 1, :]
    holders = iota((16, 8, 128), 0) * DP + d
    held = (jnp.broadcast_to(sources[None], (16, 8, 128)) == holders).reshape(128, 128)
    packed_at = slot_column(
        held, jnp.broadcast_to(position[None], (16, 8, 128)).reshape(128, 128), tri
    )
    pack[...] = jnp.where(packed_at == iota((SLOTS, cap), 1).astype(F32), 1.0, 0.0).astype(BF16)

    def chunk(h, chip, of):
        return gathered.at[h, chip, pl.ds(pl.multiple_of(of * cap, 16), cap), :]

    def ring(h, kind, chip, to):
        part = chunk(h, chip, core)
        return pltpu.make_async_remote_copy(
            src_ref=part,
            dst_ref=part,
            send_sem=ring_send.at[h, kind],
            recv_sem=ring_recv.at[h, kind],
            device_id=(e, to),
            device_id_type=MESH,
        )

    lx, rx, ox = (x + 3) % 4, (x + 1) % 4, (x + 2) % 4

    def copies(h):
        return dict(
            to_right=ring(h, 0, x, right),
            to_left=ring(h, 1, x, left),
            to_other=ring(h, 2, x, other),
            onward=ring(h, 3, lx, right) if h == 0 else ring(h, 3, rx, left),
            left_to_other=ring(h, 4, lx, other),
            right_to_other=ring(h, 5, rx, other),
            far_to_other=ring(h, 6, ox, other),
        )

    moves = [copies(0), copies(1)]

    for h in range(2):

        @pl.loop(1, 16)
        def _(k, h=h):
            s1_copy(h, k).wait_recv()

        gathered[h, x, pl.ds(pl.multiple_of(core * cap, 16), cap), :] = matmul_tn(
            pack[...], recv[h]
        ).astype(BF16)
        for name in ("to_right", "to_left", "to_other"):
            moves[h][name].start()

    @pl.loop(1, 8)
    def _(k):
        gate_copy(k).wait_recv()

    gate_row = jnp.concatenate([all_gates[b, 0:1, :] for b in range(8)], axis=1)
    load_w.wait()

    moves[0]["to_right"].wait_recv()
    moves[0]["onward"].start()
    moves[0]["left_to_other"].start()
    moves[0]["to_left"].wait_recv()
    moves[0]["right_to_other"].start()
    moves[0]["to_other"].wait_recv()
    moves[1]["to_other"].wait_recv()

    slice_d = pl.ds(pl.multiple_of(d * 256, 256), 256)
    my_place = place[:, pl.ds(pl.multiple_of(d * 128, 128), 128)]

    def compute(chip, first, gate_grad):
        row = chip * 2 * cap + iota((2 * cap, 1), 0)
        hits = place[...] == row.astype(F32)
        gate = jnp.sum(jnp.where(hits, gate_row, 0.0), axis=1, keepdims=True)
        dots = jnp.zeros((2 * cap, 1), F32)
        for start, width in TILES:
            gate_pre = matmul(gathered[0, chip], w[:, start : start + width])
            up = matmul(gathered[0, chip], w[:, H + start : H + start + width])
            u = matmul(gathered[1, chip], w[:, 2 * H + start : 2 * H + start + width])
            s = 1.0 / (1.0 + jnp.exp(-gate_pre))
            active = gate_pre * s
            hidden = active * up
            dots += jnp.sum(hidden.astype(BF16).astype(F32) * u, axis=1, keepdims=True)
            hidden_grad = gate * u
            joint[:, start : start + width] = (
                hidden_grad * up * s * (1.0 + gate_pre * (1.0 - s))
            ).astype(BF16)
            joint[:, H + start : H + start + width] = (hidden_grad * active).astype(BF16)
            joint[:, 2 * H + start : 2 * H + start + width] = (gate * hidden).astype(BF16)
        for part, (low, high) in ((0, (0, 2 * H)), (1, (2 * H, 3 * H))):
            rows_in = gathered[part, chip, :, slice_d]
            for at in range(low, high, 704):
                more = matmul_tn(rows_in, joint[:, at : at + 704])
                if first:
                    acc[:, at : at + 704] = more
                else:
                    acc[:, at : at + 704] += more
        found = my_place == row.astype(F32)
        return gate_grad + jnp.sum(jnp.where(found, dots, 0.0), axis=0, keepdims=True)

    gate_grad = compute(x, True, jnp.zeros((1, 128), F32))

    own_joint = joint.at[pl.ds(pl.multiple_of(core * cap, 16), cap), :]
    for at in range(0, D, 256):
        own_rows[:, at : at + 256] = matmul_nt(
            own_joint[:, : 2 * H], w[at : at + 256, : 2 * H]
        ).astype(BF16)
    back_send[...] = matmul(pack[...], own_rows[...]).astype(BF16)

    def back_copy(k):
        return pltpu.make_async_remote_copy(
            src_ref=block(back_send, peer(k)),
            dst_ref=block(back_recv, e),
            send_sem=back_send_sem.at[k],
            recv_sem=back_recv_sem.at[k],
            device_id=(peer(k), d),
            device_id_type=MESH,
        )

    @pl.loop(1, 16)
    def _(k):
        back_copy(k).start()

    own = pl.ds(pl.multiple_of(e * 16, 16), 16)
    back_recv[own, :] = back_send[own, :]

    moves[1]["to_left"].wait_recv()
    moves[1]["onward"].start()
    moves[1]["right_to_other"].start()
    moves[1]["to_right"].wait_recv()
    moves[1]["left_to_other"].start()

    moves[0]["left_to_other"].wait_recv()
    moves[1]["left_to_other"].wait_recv()
    gate_grad = compute(lx, False, gate_grad)
    moves[0]["right_to_other"].wait_recv()
    moves[1]["right_to_other"].wait_recv()
    gate_grad = compute(rx, False, gate_grad)

    for h in range(2):
        moves[h]["onward"].wait_recv()
        moves[h]["far_to_other"].start()

    @pl.loop(1, 16)
    def _(k):
        back_copy(k).wait_recv()

    token_out[...] = matmul_tn(sel[...], back_recv[...]).astype(BF16)

    for h in range(2):
        moves[h]["far_to_other"].wait_recv()
    gate_grad = compute(ox, False, gate_grad)
    weight_out[...] = acc[...].astype(BF16)
    gate_out[...] = gate_grad

    for h in range(2):

        @pl.loop(1, 16)
        def _(k, h=h):
            s1_copy(h, k).wait_send()

        for copy in moves[h].values():
            copy.wait_send()

    @pl.loop(1, 8)
    def _(k):
        gate_copy(k).wait_send()

    @pl.loop(1, 16)
    def _(k):
        back_copy(k).wait_send()


def layer(cap, number, picks, gates, tokens, grads, matrix):
    vmem = pl.BlockSpec(memory_space=pltpu.VMEM)
    dma = pltpu.SemaphoreType.DMA
    return pl.pallas_call(
        functools.partial(kernel, cap),
        name=f"moe_backward_{cap}",
        out_shape=(
            jax.ShapeDtypeStruct((TOK, D), BF16),
            jax.ShapeDtypeStruct((D // DP, 3 * H), BF16),
            jax.ShapeDtypeStruct((1, ROWS), F32),
        ),
        in_specs=[vmem, vmem, vmem, vmem, pl.BlockSpec(memory_space=pl.ANY)],
        out_specs=(vmem, vmem, vmem),
        scratch_shapes=[
            pltpu.VMEM((D, 3 * H), BF16),
            pltpu.VMEM((2, SLOTS, D), BF16),
            pltpu.VMEM((2, SLOTS, D), BF16),
            pltpu.VMEM((2, 4, 2 * cap, D), BF16),
            pltpu.VMEM((2 * cap, 3 * H), BF16),
            pltpu.VMEM((D // DP, 3 * H), F32),
            pltpu.VMEM((SLOTS, D), BF16),
            pltpu.VMEM((SLOTS, D), BF16),
            pltpu.VMEM((SLOTS, TOK), BF16),
            pltpu.VMEM((SLOTS, cap), BF16),
            pltpu.VMEM((cap, D), BF16),
            pltpu.VMEM((1, 8 * ROWS), F32),
            pltpu.VMEM((8, 8, ROWS), F32),
            dma,
            dma((2, 16)),
            dma((2, 16)),
            dma((8,)),
            dma((8,)),
            dma((2, 7)),
            dma((2, 7)),
            dma((16,)),
            dma((16,)),
        ],
        compiler_params=pltpu.CompilerParams(
            collective_id=number, has_side_effects=True, vmem_limit_bytes=62 * 2**20
        ),
    )(picks, gates, tokens, grads, matrix)


def shards(tokens, out_grad, weights, gate_values, expert_picks):
    planes = (expert_picks >> 8) & 7
    counts = jnp.sum(
        (planes[:, :, None] == jnp.arange(DP, dtype=I32)[None, None, :]).astype(I32), axis=1
    )
    picks = expert_picks.reshape(EXPERTS * DP, ROWS)
    operands = (picks, gate_values, tokens, out_grad, weights[0])
    token_grad, weight_grad, gate_grad = lax.cond(
        jnp.max(counts) <= 160,
        functools.partial(layer, 160, 0),
        functools.partial(layer, 256, 1),
        *operands,
    )
    return token_grad, weight_grad[None], gate_grad


def solution(mesh):
    return jax.shard_map(
        shards,
        mesh=mesh,
        in_specs=(
            P(("expert", "dp"), None),
            P(("expert", "dp"), None),
            P("expert", None, None),
            P("expert", "dp"),
            P(),
        ),
        out_specs=(P(("expert", "dp"), None), P("expert", "dp", None), P("expert", "dp")),
        check_vma=False,
    )
```

```python
import functools

import jax
import jax.numpy as jnp
from jax import lax
from jax.experimental import pallas as pl
from jax.experimental.pallas import tpu as pltpu
from jax.sharding import PartitionSpec as P

MESH = pl.DeviceIdType.MESH
F32 = jnp.float32
BF16 = jnp.bfloat16
I32 = jnp.int32
D = 2048
H = 1408
EXPERTS = 16
DP = 8
TOK = 256
SLOTS = 256
ROWS = 128
TILES = H // 128
HALF = D // 2


def iota(shape, axis):
    return lax.broadcasted_iota(I32, shape, axis)


def matmul(a, b):
    return jnp.dot(a, b, preferred_element_type=F32)


def matmul_tn(a, b):
    return lax.dot_general(a, b, (((0,), (0,)), ((), ())), preferred_element_type=F32)


def matmul_nt(a, b):
    return lax.dot_general(a, b, (((1,), (1,)), ((), ())), preferred_element_type=F32)


def slot_column(mask, values, tri):
    ones = jnp.where(mask, 1.0, 0.0)
    rank = matmul(ones.astype(BF16), tri) * ones
    rank3 = rank.reshape(16, 8, 128)
    value3 = values.reshape(16, 8, 128)
    ranks = jnp.concatenate([rank3, rank3], axis=1).reshape(SLOTS, 128)
    twice = jnp.concatenate([value3, value3], axis=1).reshape(SLOTS, 128)
    wanted = ((iota((SLOTS, 128), 0) // 8) % 2 + 1).astype(F32)
    return jnp.sum(jnp.where(ranks == wanted, twice + 1.0, 0.0), axis=1, keepdims=True) - 1.0


def kernel(
    cap,
    all_picks_ref,
    gates_ref,
    tok_ref,
    grad_ref,
    w_hbm,
    token_out,
    weight_out,
    gate_out,
    most_out,
    w,
    send,
    recv,
    gathered,
    gate_up,
    joint,
    acc,
    back_send,
    back_recv,
    sel,
    pack,
    own_rows,
    picks_ref,
    place,
    all_gates,
    w_sem,
    s1_send,
    s1_recv,
    gate_send,
    gate_recv,
    ring_send,
    ring_recv,
    back_send_sem,
    back_recv_sem,
):
    e = lax.axis_index("expert")
    d = lax.axis_index("dp")
    ey, ez = e // 4, e % 4
    x, core = d // 2, d % 2
    me = e * DP + d
    right = ((x + 1) % 4) * 2 + core
    left = ((x + 3) % 4) * 2 + core
    other = x * 2 + 1 - core

    def load_part(n, half):
        return pltpu.make_async_copy(
            w_hbm.at[:, pl.ds(pl.multiple_of(half * H + n * 128, 128), 128)],
            w.at[:, pl.ds(pl.multiple_of(n * 256 + half * 128, 128), 128)],
            w_sem.at[n * 2 + half],
        )

    load_down = pltpu.make_async_copy(
        w_hbm.at[:, 2 * H : 3 * H], w.at[:, 2 * H : 3 * H], w_sem.at[2 * TILES]
    )

    @pl.loop(0, TILES)
    def _(n):
        load_part(n, 0).start()
        load_part(n, 1).start()

    load_down.start()

    def peer(k):
        return ((ey + k // 4) % 4) * 4 + (ez + k % 4) % 4

    barrier = pltpu.get_barrier_semaphore()

    @pl.loop(1, 16)
    def _(k):
        pl.semaphore_signal(barrier, inc=1, device_id=(peer(k), d), device_id_type=MESH)

    @pl.loop(1, 8)
    def _(k):
        pl.semaphore_signal(barrier, inc=1, device_id=(e, (d + k) % 8), device_id_type=MESH)

    tri = jnp.where(iota((128, 128), 0) <= iota((128, 128), 1), 1.0, 0.0).astype(BF16)
    picks_ref[...] = all_picks_ref[...].reshape(EXPERTS * DP, ROWS)
    picks = picks_ref[...]
    token_of = slot_column((picks >> 8) == me, (picks & 255).astype(F32), tri)
    sel[...] = jnp.where(token_of == iota((SLOTS, TOK), 1).astype(F32), 1.0, 0.0).astype(BF16)
    all_gates[d] = jnp.broadcast_to(gates_ref[...], (8, 128))

    def block(ref, row):
        return ref.at[pl.ds(pl.multiple_of(row * 16, 16), 16), :]

    def columns(q):
        return slice((q % 2) * HALF, (q % 2) * HALF + HALF)

    def s1_copy(q, k):
        return pltpu.make_async_remote_copy(
            src_ref=block(send.at[q // 2], peer(k)).at[:, columns(q)],
            dst_ref=block(recv.at[q // 2], e).at[:, columns(q)],
            send_sem=s1_send.at[q, k],
            recv_sem=s1_recv.at[q, k],
            device_id=(peer(k), d),
            device_id_type=MESH,
        )

    def gate_copy(k):
        return pltpu.make_async_remote_copy(
            src_ref=all_gates.at[d],
            dst_ref=all_gates.at[d],
            send_sem=gate_send.at[k],
            recv_sem=gate_recv.at[k],
            device_id=(e, (d + k) % 8),
            device_id_type=MESH,
        )

    own = pl.ds(pl.multiple_of(e * 16, 16), 16)
    for q in range(4):
        ref = (tok_ref, grad_ref)[q // 2]
        send[q // 2, :, columns(q)] = matmul(sel[...], ref[:, columns(q)]).astype(BF16)
        if q == 0:
            pl.semaphore_wait(barrier, 22)

        @pl.loop(1, 16)
        def _(k, q=q):
            s1_copy(q, k).start()

        recv[q // 2, own, columns(q)] = send[q // 2, own, columns(q)]

    @pl.loop(1, 8)
    def _(k):
        gate_copy(k).start()

    mine = picks_ref[pl.ds(pl.multiple_of(e * 8, 8), 8), :]
    sources = mine >> 8
    planes = sources & 7
    before = jnp.zeros((8, 1), F32)
    positions = []
    for b in range(8):
        hit = jnp.where(
            jnp.broadcast_to(planes[b : b + 1, :], (8, 128)) == iota((8, 128), 0), 1.0, 0.0
        )
        count = matmul(hit.astype(BF16), tri)
        positions.append(jnp.sum(hit * (count + before), axis=0, keepdims=True) - 1.0)
        before = before + count[:, 127:128]
    position = jnp.concatenate(positions, axis=0)
    rows_of = position + planes.astype(F32) * cap
    for b in range(8):
        place[:, b * 128 : (b + 1) * 128] = rows_of[b : b + 1, :]
    holders = iota((16, 8, 128), 0) * DP + d
    held = (jnp.broadcast_to(sources[None], (16, 8, 128)) == holders).reshape(128, 128)
    packed_at = slot_column(
        held, jnp.broadcast_to(position[None], (16, 8, 128)).reshape(128, 128), tri
    )
    pack[...] = jnp.where(packed_at == iota((SLOTS, cap), 1).astype(F32), 1.0, 0.0).astype(BF16)

    most = jnp.zeros((16, 1), F32)
    planes_of = (picks >> 8) & 7
    for plane in range(8):
        counts = jnp.sum(jnp.where(planes_of == plane, 1.0, 0.0), axis=1, keepdims=True)
        most = jnp.maximum(most, jnp.sum(counts.reshape(16, 8, 1), axis=1))
    most_out[0, 0] = jnp.max(most)

    lx, rx, ox = (x + 3) % 4, (x + 1) % 4, (x + 2) % 4

    def ring(q, kind, chip, to):
        rows = pl.ds(pl.multiple_of(core * cap, 16), cap)
        part = gathered.at[q // 2, chip, rows, columns(q)]
        return pltpu.make_async_remote_copy(
            src_ref=part,
            dst_ref=part,
            send_sem=ring_send.at[q, kind],
            recv_sem=ring_recv.at[q, kind],
            device_id=(e, to),
            device_id_type=MESH,
        )

    def to_right(q):
        return ring(q, 0, x, right)

    def to_left(q):
        return ring(q, 1, x, left)

    def to_other(q):
        return ring(q, 2, x, other)

    def onward(q):
        return ring(q, 3, lx, right) if q % 2 == 0 else ring(q, 3, rx, left)

    def left_to_other(q):
        return ring(q, 4, lx, other)

    def right_to_other(q):
        return ring(q, 5, rx, other)

    def far_to_other(q):
        return ring(q, 6, ox, other)

    def enter(q):
        @pl.loop(1, 16)
        def _(k):
            s1_copy(q, k).wait_recv()

        rows = pl.ds(pl.multiple_of(core * cap, 16), cap)
        gathered[q // 2, x, rows, columns(q)] = matmul_tn(
            pack[...], recv[q // 2, :, columns(q)]
        ).astype(BF16)
        to_right(q).start()
        to_left(q).start()
        to_other(q).start()

    def forward(q):
        to_right(q).wait_recv()
        to_left(q).wait_recv()
        onward(q).start()
        left_to_other(q).start()
        right_to_other(q).start()

    def forward_far(q):
        onward(q).wait_recv()
        far_to_other(q).start()

    slice_d = pl.ds(pl.multiple_of(d * 256, 256), 256)
    my_place = place[:, pl.ds(pl.multiple_of(d * 128, 128), 128)]

    def chip_at(j):
        hop = (j + 1) // 2
        return (x + hop + (j % 2) * (4 - 2 * hop)) % 4

    def project(j):
        chip, slot = chip_at(j), j % 3
        for n in range(TILES):
            gate_up[slot, :, n * 256 : n * 256 + 256] = matmul(
                gathered[0, chip], w[:, n * 256 : n * 256 + 256]
            )

    def finish(j):
        chip, slot = chip_at(j), j % 3
        row = (chip * 2 * cap + iota((2 * cap, 1), 0)).astype(F32)
        gate_row = jnp.concatenate([all_gates[b, 0:1, :] for b in range(8)], axis=1)
        gate = jnp.sum(jnp.where(place[...] == row, gate_row, 0.0), axis=1, keepdims=True)
        dots = jnp.zeros((2 * cap, 128), F32)
        token_rows = gathered[0, chip, :, slice_d].T
        grad_rows = gathered[1, chip, :, slice_d].T

        def upstream(n):
            low = 2 * H + n * 256
            return matmul(gathered[1, chip], w[:, low : min(low + 256, 3 * H)])

        def add_up(rows, low, high):
            acc[:, low:high] += matmul(rows, joint[:, low:high])

        following = upstream(0)
        for n in range(TILES):
            if n % 2 == 0:
                u = following
                if n // 2 + 1 < (TILES + 1) // 2:
                    following = upstream(n // 2 + 1)
            part = u[:, (n % 2) * 128 : (n % 2) * 128 + 128]
            gate_pre = gate_up[slot, :, n * 256 : n * 256 + 128]
            up = gate_up[slot, :, n * 256 + 128 : n * 256 + 256]
            s = 0.5 + 0.5 * jnp.tanh(0.5 * gate_pre)
            active = gate_pre * s
            hidden = active * up
            dots += hidden.astype(BF16).astype(F32) * part
            hidden_grad = gate * part
            joint[:, n * 256 : n * 256 + 128] = (
                hidden_grad * up * s * (1.0 + gate_pre * (1.0 - s))
            ).astype(BF16)
            joint[:, n * 256 + 128 : n * 256 + 256] = (hidden_grad * active).astype(BF16)
            joint[:, 2 * H + n * 128 : 2 * H + n * 128 + 128] = (gate * hidden).astype(BF16)
            if n > 0:
                add_up(token_rows, n * 256 - 256, n * 256)
            if n % 2 == 0 and n > 0:
                add_up(grad_rows, 2 * H + n * 128 - 256, 2 * H + n * 128)
        add_up(token_rows, 2 * H - 256, 2 * H)
        add_up(grad_rows, 3 * H - 128, 3 * H)
        found = my_place == row
        gate_out[...] += jnp.sum(
            jnp.where(found, jnp.sum(dots, axis=1, keepdims=True), 0.0), axis=0, keepdims=True
        )

    def back_copy(k):
        return pltpu.make_async_remote_copy(
            src_ref=block(back_send, peer(k)),
            dst_ref=block(back_recv, e),
            send_sem=back_send_sem.at[k],
            recv_sem=back_recv_sem.at[k],
            device_id=(peer(k), d),
            device_id_type=MESH,
        )

    def send_back():
        own_joint = joint.at[pl.ds(pl.multiple_of(core * cap, 16), cap), :]
        for at in range(0, D, 256):
            own_rows[:, at : at + 256] = matmul_nt(
                own_joint[:, : 2 * H], w[at : at + 256, : 2 * H]
            ).astype(BF16)
        back_send[...] = matmul(pack[...], own_rows[...]).astype(BF16)

        @pl.loop(1, 16)
        def _(k):
            back_copy(k).start()

        back_recv[own, :] = back_send[own, :]

    def combine():
        @pl.loop(1, 16)
        def _(k):
            back_copy(k).wait_recv()

        token_out[...] = matmul_tn(sel[...], back_recv[...]).astype(BF16)

    gate_out[...] = jnp.zeros((1, 128), F32)
    acc[...] = jnp.zeros(acc.shape, F32)
    enter(0)
    enter(1)
    forward(0)

    @pl.loop(1, 8)
    def _(k):
        gate_copy(k).wait_recv()

    @pl.loop(0, TILES)
    def _(n):
        load_part(n, 0).wait()
        load_part(n, 1).wait()

    load_down.wait()
    to_other(0).wait_recv()
    to_other(1).wait_recv()

    @pl.loop(0, 8)
    def _(t):
        @pl.when(t == 1)
        def _():
            enter(2)
            forward(1)
            enter(3)
            left_to_other(0).wait_recv()
            left_to_other(1).wait_recv()

        @pl.when(t == 2)
        def _():
            to_other(2).wait_recv()
            to_other(3).wait_recv()

        @pl.when(t == 3)
        def _():
            forward(2)
            right_to_other(0).wait_recv()
            right_to_other(1).wait_recv()

        @pl.when(t == 4)
        def _():
            forward_far(0)
            send_back()
            forward_far(1)
            forward(3)
            far_to_other(0).wait_recv()
            far_to_other(1).wait_recv()

        @pl.when(t == 5)
        def _():
            left_to_other(2).wait_recv()
            left_to_other(3).wait_recv()

        @pl.when(t == 6)
        def _():
            forward_far(2)
            right_to_other(2).wait_recv()
            right_to_other(3).wait_recv()

        @pl.when(t == 7)
        def _():
            forward_far(3)
            combine()
            far_to_other(2).wait_recv()
            far_to_other(3).wait_recv()

        finishing = (t == 2) | (t >= 5)

        @pl.when(jnp.logical_not(finishing))
        def _():
            project(t - t // 3)

        @pl.when(finishing)
        def _():
            finish((t // 5) * (t - 4))

    for n in range(TILES):
        for part in range(2):
            weight_out[:, part * H + n * 128 : part * H + n * 128 + 128] = acc[
                :, n * 256 + part * 128 : n * 256 + part * 128 + 128
            ].astype(BF16)
    weight_out[:, 2 * H :] = acc[:, 2 * H :].astype(BF16)

    for q in range(4):

        @pl.loop(1, 16)
        def _(k, q=q):
            s1_copy(q, k).wait_send()

        for copy in (
            to_right,
            to_left,
            to_other,
            onward,
            left_to_other,
            right_to_other,
            far_to_other,
        ):
            copy(q).wait_send()

    @pl.loop(1, 8)
    def _(k):
        gate_copy(k).wait_send()

    @pl.loop(1, 16)
    def _(k):
        back_copy(k).wait_send()


def layer(cap, picks, gates, tokens, grads, matrix):
    vmem = pl.BlockSpec(memory_space=pltpu.VMEM)
    dma = pltpu.SemaphoreType.DMA
    return pl.pallas_call(
        functools.partial(kernel, cap),
        name=f"moe_backward_{cap}",
        out_shape=(
            jax.ShapeDtypeStruct((TOK, D), BF16),
            jax.ShapeDtypeStruct((D // DP, 3 * H), BF16),
            jax.ShapeDtypeStruct((1, ROWS), F32),
            jax.ShapeDtypeStruct((1, 1), F32),
        ),
        in_specs=[vmem, vmem, vmem, vmem, pl.BlockSpec(memory_space=pl.ANY)],
        out_specs=(vmem, vmem, vmem, pl.BlockSpec(memory_space=pltpu.SMEM)),
        scratch_shapes=[
            pltpu.VMEM((D, 3 * H), BF16),
            pltpu.VMEM((2, SLOTS, D), BF16),
            pltpu.VMEM((2, SLOTS, D), BF16),
            pltpu.VMEM((2, 4, 2 * cap, D), BF16),
            pltpu.VMEM((3, 2 * cap, 2 * H), F32),
            pltpu.VMEM((2 * cap, 3 * H), BF16),
            pltpu.VMEM((D // DP, 3 * H), F32),
            pltpu.VMEM((SLOTS, D), BF16),
            pltpu.VMEM((SLOTS, D), BF16),
            pltpu.VMEM((SLOTS, TOK), BF16),
            pltpu.VMEM((SLOTS, cap), BF16),
            pltpu.VMEM((cap, D), BF16),
            pltpu.VMEM((EXPERTS * DP, ROWS), I32),
            pltpu.VMEM((1, 8 * ROWS), F32),
            pltpu.VMEM((8, 8, ROWS), F32),
            dma((2 * TILES + 1,)),
            dma((4, 16)),
            dma((4, 16)),
            dma((8,)),
            dma((8,)),
            dma((4, 7)),
            dma((4, 7)),
            dma((16,)),
            dma((16,)),
        ],
        compiler_params=pltpu.CompilerParams(
            collective_id=0, has_side_effects=True, vmem_limit_bytes=62 * 2**20
        ),
    )(picks, gates, tokens, grads, matrix)


def expert_pass(inputs, upstream, scales, matrix):
    hidden_width = matrix.shape[1] // 3
    gate_up = matrix[:, : 2 * hidden_width]
    down_proj = matrix[:, 2 * hidden_width :]
    projected = jnp.dot(inputs, gate_up, preferred_element_type=jnp.float32)
    gate_pre = projected[:, :hidden_width]
    up_values = projected[:, hidden_width:]
    logistic = jax.nn.sigmoid(gate_pre)
    activated = gate_pre * logistic
    hidden = (activated * up_values).astype(jnp.bfloat16)
    contract = (((1,), (1,)), ((), ()))
    output = lax.dot_general(hidden, down_proj, contract, preferred_element_type=jnp.float32)
    gate_grad = jnp.sum(upstream.astype(jnp.float32) * output, axis=1)
    scaled = (scales[:, None] * upstream.astype(jnp.float32)).astype(jnp.bfloat16)
    hidden_grad = jnp.dot(scaled, down_proj, preferred_element_type=jnp.float32)
    pre_grad = (hidden_grad * up_values * logistic * (1.0 + gate_pre * (1.0 - logistic))).astype(
        jnp.bfloat16
    )
    up_grad = (hidden_grad * activated).astype(jnp.bfloat16)
    joint_grad = jnp.concatenate([pre_grad, up_grad], axis=1)
    token_part = lax.dot_general(joint_grad, gate_up, contract, preferred_element_type=jnp.float32)
    return (token_part, gate_grad, joint_grad, hidden, scaled)


def any_load(tokens, out_grad, weights, gate_values, expert_picks):
    expert_count = lax.axis_size("expert")
    data_count = lax.axis_size("dp")
    holders = expert_count * data_count
    tok_rows = tokens.shape[0]
    width = tokens.shape[1]
    capacity = expert_picks.shape[1]
    rows = capacity // data_count
    slots = 2 * rows // holders
    total_slots = holders * slots
    expert_index = lax.axis_index("expert")
    data_index = lax.axis_index("dp")
    owner_index = expert_index * data_count + data_index
    contract_rows = (((0,), (0,)), ((), ()))
    sources = expert_picks // tok_rows
    held_here = (sources == owner_index).reshape(expert_picks.shape[0], data_count, rows)
    upto = jnp.arange(rows)[:, None] <= jnp.arange(rows)[None, :]
    ranks = matmul(held_here.astype(BF16), upto.astype(BF16)).astype(jnp.int32) - 1
    targets = (
        jnp.arange(expert_picks.shape[0], dtype=jnp.int32)[:, None, None] * data_count
        + jnp.arange(data_count, dtype=jnp.int32)[None, :, None]
    )
    positions = jnp.where(held_here, targets * slots + ranks, total_slots)
    local_rows = (expert_picks - owner_index * tok_rows).reshape(positions.shape)
    slot_table = (
        jnp.full((total_slots,), tok_rows, jnp.int32)
        .at[positions.reshape(-1)]
        .set(local_rows.reshape(-1), mode="drop")
    )
    zero_row = jnp.zeros((1, width), jnp.bfloat16)
    send_tokens = jnp.concatenate([tokens, zero_row], axis=0)[slot_table].reshape(
        holders, slots, width
    )
    send_grads = jnp.concatenate([out_grad, zero_row], axis=0)[slot_table].reshape(
        holders, slots, width
    )
    got_tokens, got_grads = (
        lax.all_to_all(send_tokens, ("expert", "dp"), split_axis=0, concat_axis=0, tiled=True),
        lax.all_to_all(send_grads, ("expert", "dp"), split_axis=0, concat_axis=0, tiled=True),
    )
    flat_tokens = got_tokens.reshape(total_slots, width)
    flat_grads = got_grads.reshape(total_slots, width)
    own_picks = lax.dynamic_slice(expert_picks, (expert_index, data_index * rows), (1, rows))[0]
    pick_sources = own_picks // tok_rows
    steps_index = jnp.arange(rows, dtype=jnp.int32)
    earlier = steps_index[:, None] > steps_index[None, :]
    same_source = pick_sources[:, None] == pick_sources[None, :]
    pick_ranks = jnp.sum((earlier & same_source).astype(jnp.int32), axis=1)
    pick_slots = pick_sources * slots + pick_ranks
    scales = gate_values[0]
    matrix = weights[0]
    inputs = flat_tokens[pick_slots]
    upstream = flat_grads[pick_slots]
    token_part, gate_grad, joint_grad, hidden, scaled = expert_pass(
        inputs, upstream, scales, matrix
    )
    back_rows = jnp.zeros((total_slots, width), jnp.float32).at[pick_slots].set(token_part)
    left_part = lax.dot_general(
        inputs, joint_grad, contract_rows, preferred_element_type=jnp.float32
    )
    right_part = lax.dot_general(scaled, hidden, contract_rows, preferred_element_type=jnp.float32)
    parts = jnp.concatenate([left_part, right_part], axis=1).reshape(data_count, -1, 3 * H)
    summed = jnp.sum(lax.all_to_all(parts, "dp", split_axis=0, concat_axis=0, tiled=True), axis=0)
    weight_grad = summed.astype(jnp.bfloat16)[None]
    returned = lax.all_to_all(
        back_rows.reshape(holders, slots, width),
        ("expert", "dp"),
        split_axis=0,
        concat_axis=0,
        tiled=True,
    )
    token_sum = (
        jnp.zeros((tok_rows + 1, width), jnp.float32)
        .at[slot_table]
        .add(returned.reshape(total_slots, width))
    )
    token_grad = token_sum[:tok_rows].astype(jnp.bfloat16)
    return (token_grad, weight_grad, gate_grad[None])


def copy_kernel(token_in, weight_in, gate_in, token_out, weight_out, gate_out, sems):
    moves = [
        pltpu.make_async_copy(token_in, token_out, sems.at[0]),
        pltpu.make_async_copy(weight_in, weight_out, sems.at[1]),
        pltpu.make_async_copy(gate_in, gate_out, sems.at[2]),
    ]
    for move in moves:
        move.start()
    for move in moves:
        move.wait()


def hand_over(*made):
    anywhere = pl.BlockSpec(memory_space=pl.ANY)
    return tuple(
        pl.pallas_call(
            copy_kernel,
            name="hand_over",
            out_shape=[jax.ShapeDtypeStruct(m.shape, m.dtype) for m in made],
            in_specs=[pl.BlockSpec(memory_space=pltpu.VMEM)] * 3,
            out_specs=[anywhere] * 3,
            scratch_shapes=[pltpu.SemaphoreType.DMA((3,))],
        )(*made)
    )


CAP = 160


def shards(tokens, out_grad, weights, gate_values, expert_picks):
    *made, most = layer(CAP, expert_picks, gate_values, tokens, out_grad, weights[0])
    given = (tokens, out_grad, weights, gate_values, expert_picks)

    def otherwise(made, given):
        token_grad, weight_grad, gate_grad = any_load(*given)
        return token_grad, weight_grad[0], gate_grad

    token_grad, weight_grad, gate_grad = lax.cond(
        most[0, 0] <= CAP, lambda made, given: hand_over(*made), otherwise, made, given
    )
    return token_grad, weight_grad[None], gate_grad


def solution(mesh):
    return jax.shard_map(
        shards,
        mesh=mesh,
        in_specs=(
            P(("expert", "dp"), None),
            P(("expert", "dp"), None),
            P("expert", None, None),
            P("expert", "dp"),
            P(),
        ),
        out_specs=(P(("expert", "dp"), None), P("expert", "dp", None), P("expert", "dp")),
        check_vma=False,
    )
```

```python
import functools

import jax
import jax.numpy as jnp
from jax import lax
from jax.experimental import pallas as pl
from jax.experimental.pallas import tpu as pltpu
from jax.sharding import PartitionSpec as P

MESH = pl.DeviceIdType.MESH
F32 = jnp.float32
BF16 = jnp.bfloat16
I32 = jnp.int32
D = 2048
H = 1408
EXPERTS = 16
DP = 8
TOK = 256
SLOTS = 256
ROWS = 128
TILES = H // 128
HALF = D // 2


def iota(shape, axis):
    return lax.broadcasted_iota(I32, shape, axis)


def matmul(a, b):
    return jnp.dot(a, b, preferred_element_type=F32)


def matmul_tn(a, b):
    return lax.dot_general(a, b, (((0,), (0,)), ((), ())), preferred_element_type=F32)


def matmul_nt(a, b):
    return lax.dot_general(a, b, (((1,), (1,)), ((), ())), preferred_element_type=F32)


def slot_column(mask, values, tri):
    ones = jnp.where(mask, 1.0, 0.0)
    rank = matmul(ones.astype(BF16), tri) * ones
    rank3 = rank.reshape(16, 8, 128)
    value3 = values.reshape(16, 8, 128)
    ranks = jnp.concatenate([rank3, rank3], axis=1).reshape(SLOTS, 128)
    twice = jnp.concatenate([value3, value3], axis=1).reshape(SLOTS, 128)
    wanted = ((iota((SLOTS, 128), 0) // 8) % 2 + 1).astype(F32)
    return jnp.sum(jnp.where(ranks == wanted, twice + 1.0, 0.0), axis=1, keepdims=True) - 1.0


def kernel(
    cap,
    all_picks_ref,
    gates_ref,
    tok_ref,
    grad_ref,
    w_hbm,
    token_out,
    weight_out,
    gate_out,
    most_out,
    w,
    send,
    recv,
    gathered,
    gate_up,
    joint,
    acc,
    sel,
    pack,
    own_rows,
    picks_ref,
    place,
    all_gates,
    w_sem,
    s1_send,
    s1_recv,
    gate_send,
    gate_recv,
    ring_send,
    ring_recv,
    back_send_sem,
    back_recv_sem,
):
    e = lax.axis_index("expert")
    d = lax.axis_index("dp")
    ey, ez = e // 4, e % 4
    x, core = d // 2, d % 2
    me = e * DP + d
    right = ((x + 1) % 4) * 2 + core
    left = ((x + 3) % 4) * 2 + core
    other = x * 2 + 1 - core

    def load_part(n, half):
        return pltpu.make_async_copy(
            w_hbm.at[:, pl.ds(pl.multiple_of(half * H + n * 128, 128), 128)],
            w.at[:, pl.ds(pl.multiple_of(n * 256 + half * 128, 128), 128)],
            w_sem.at[n * 2 + half],
        )

    load_down = pltpu.make_async_copy(
        w_hbm.at[:, 2 * H : 3 * H], w.at[:, 2 * H : 3 * H], w_sem.at[2 * TILES]
    )

    @pl.loop(0, TILES)
    def _(n):
        load_part(n, 0).start()
        load_part(n, 1).start()

    load_down.start()

    def peer(k):
        return ((ey + k // 4) % 4) * 4 + (ez + k % 4) % 4

    barrier = pltpu.get_barrier_semaphore()

    @pl.loop(1, 16)
    def _(k):
        pl.semaphore_signal(barrier, inc=1, device_id=(peer(k), d), device_id_type=MESH)

    @pl.loop(1, 8)
    def _(k):
        pl.semaphore_signal(barrier, inc=1, device_id=(e, (d + k) % 8), device_id_type=MESH)

    tri = jnp.where(iota((128, 128), 0) <= iota((128, 128), 1), 1.0, 0.0).astype(BF16)
    picks_ref[...] = all_picks_ref[...].reshape(EXPERTS * DP, ROWS)
    picks = picks_ref[...]
    token_of = slot_column((picks >> 8) == me, (picks & 255).astype(F32), tri)
    sel[...] = jnp.where(token_of == iota((SLOTS, TOK), 1).astype(F32), 1.0, 0.0).astype(BF16)
    all_gates[d] = jnp.broadcast_to(gates_ref[...], (8, 128))

    def block(ref, row):
        return ref.at[pl.ds(pl.multiple_of(row * 16, 16), 16), :]

    def columns(q):
        return slice((q % 2) * HALF, (q % 2) * HALF + HALF)

    def s1_copy(q, k):
        return pltpu.make_async_remote_copy(
            src_ref=block(send.at[q // 2], peer(k)).at[:, columns(q)],
            dst_ref=block(recv.at[q // 2], e).at[:, columns(q)],
            send_sem=s1_send.at[q, k],
            recv_sem=s1_recv.at[q, k],
            device_id=(peer(k), d),
            device_id_type=MESH,
        )

    def gate_copy(k):
        return pltpu.make_async_remote_copy(
            src_ref=all_gates.at[d],
            dst_ref=all_gates.at[d],
            send_sem=gate_send.at[k],
            recv_sem=gate_recv.at[k],
            device_id=(e, (d + k) % 8),
            device_id_type=MESH,
        )

    def launch(q):
        @pl.loop(1, 16)
        def _(k):
            s1_copy(q, k).start()

    def launch_next(q):
        @pl.loop(1, 16)
        def _(k):
            s1_copy(q, k).wait_send()

        launch(q + 1)

    own = pl.ds(pl.multiple_of(e * 16, 16), 16)
    for q in range(4):
        ref = (tok_ref, grad_ref)[q // 2]
        send[q // 2, :, columns(q)] = matmul(sel[...], ref[:, columns(q)]).astype(BF16)
        if q == 0:
            pl.semaphore_wait(barrier, 22)
            launch(0)
        recv[q // 2, own, columns(q)] = send[q // 2, own, columns(q)]

    @pl.loop(1, 8)
    def _(k):
        gate_copy(k).start()

    mine = picks_ref[pl.ds(pl.multiple_of(e * 8, 8), 8), :]
    sources = mine >> 8
    planes = sources & 7
    before = jnp.zeros((8, 1), F32)
    positions = []
    for b in range(8):
        hit = jnp.where(
            jnp.broadcast_to(planes[b : b + 1, :], (8, 128)) == iota((8, 128), 0), 1.0, 0.0
        )
        count = matmul(hit.astype(BF16), tri)
        positions.append(jnp.sum(hit * (count + before), axis=0, keepdims=True) - 1.0)
        before = before + count[:, 127:128]
    position = jnp.concatenate(positions, axis=0)
    rows_of = position + planes.astype(F32) * cap
    for b in range(8):
        place[:, b * 128 : (b + 1) * 128] = rows_of[b : b + 1, :]
    holders = iota((16, 8, 128), 0) * DP + d
    held = (jnp.broadcast_to(sources[None], (16, 8, 128)) == holders).reshape(128, 128)
    packed_at = slot_column(
        held, jnp.broadcast_to(position[None], (16, 8, 128)).reshape(128, 128), tri
    )
    pack[...] = jnp.where(packed_at == iota((SLOTS, cap), 1).astype(F32), 1.0, 0.0).astype(BF16)

    most = jnp.zeros((16, 1), F32)
    planes_of = (picks >> 8) & 7
    for plane in range(8):
        counts = jnp.sum(jnp.where(planes_of == plane, 1.0, 0.0), axis=1, keepdims=True)
        most = jnp.maximum(most, jnp.sum(counts.reshape(16, 8, 1), axis=1))
    most_out[0, 0] = jnp.max(most)

    lx, rx, ox = (x + 3) % 4, (x + 1) % 4, (x + 2) % 4

    def ring(q, kind, chip, to):
        rows = pl.ds(pl.multiple_of(core * cap, 16), cap)
        part = gathered.at[q // 2, chip, rows, columns(q)]
        return pltpu.make_async_remote_copy(
            src_ref=part,
            dst_ref=part,
            send_sem=ring_send.at[q, kind],
            recv_sem=ring_recv.at[q, kind],
            device_id=(e, to),
            device_id_type=MESH,
        )

    def to_right(q):
        return ring(q, 0, x, right)

    def to_left(q):
        return ring(q, 1, x, left)

    def to_other(q):
        return ring(q, 2, x, other)

    def onward(q):
        return ring(q, 3, lx, right) if q % 2 == 0 else ring(q, 3, rx, left)

    def left_to_other(q):
        return ring(q, 4, lx, other)

    def right_to_other(q):
        return ring(q, 5, rx, other)

    def far_to_other(q):
        return ring(q, 6, ox, other)

    def enter(q):
        @pl.loop(1, 16)
        def _(k):
            s1_copy(q, k).wait_recv()

        rows = pl.ds(pl.multiple_of(core * cap, 16), cap)
        gathered[q // 2, x, rows, columns(q)] = matmul_tn(
            pack[...], recv[q // 2, :, columns(q)]
        ).astype(BF16)
        to_right(q).start()
        to_left(q).start()
        to_other(q).start()

    def forward(q):
        to_right(q).wait_recv()
        to_left(q).wait_recv()
        onward(q).start()
        left_to_other(q).start()
        right_to_other(q).start()

    def forward_far(q):
        onward(q).wait_recv()
        far_to_other(q).start()

    slice_d = pl.ds(pl.multiple_of(d * 256, 256), 256)
    my_place = place[:, pl.ds(pl.multiple_of(d * 128, 128), 128)]

    def chip_at(j):
        hop = (j + 1) // 2
        return (x + hop + (j % 2) * (4 - 2 * hop)) % 4

    def project(j):
        chip, slot = chip_at(j), j % 3
        for n in range(TILES):
            gate_up[slot, :, n * 256 : n * 256 + 256] = matmul(
                gathered[0, chip], w[:, n * 256 : n * 256 + 256]
            )

    def finish(j):
        chip, slot = chip_at(j), j % 3
        row = (chip * 2 * cap + iota((2 * cap, 1), 0)).astype(F32)
        gate_row = jnp.concatenate([all_gates[b, 0:1, :] for b in range(8)], axis=1)
        gate = jnp.sum(jnp.where(place[...] == row, gate_row, 0.0), axis=1, keepdims=True)
        dots = jnp.zeros((2 * cap, 128), F32)
        token_rows = gathered[0, chip, :, slice_d].T
        grad_rows = gathered[1, chip, :, slice_d].T

        def upstream(n):
            low = 2 * H + n * 256
            return matmul(gathered[1, chip], w[:, low : min(low + 256, 3 * H)])

        def add_up(rows, low, high):
            acc[:, low:high] += matmul(rows, joint[:, low:high])

        following = upstream(0)
        for n in range(TILES):
            if n % 2 == 0:
                u = following
                if n // 2 + 1 < (TILES + 1) // 2:
                    following = upstream(n // 2 + 1)
            part = u[:, (n % 2) * 128 : (n % 2) * 128 + 128]
            gate_pre = gate_up[slot, :, n * 256 : n * 256 + 128]
            up = gate_up[slot, :, n * 256 + 128 : n * 256 + 256]
            s = 0.5 + 0.5 * jnp.tanh(0.5 * gate_pre)
            active = gate_pre * s
            hidden = active * up
            dots += hidden.astype(BF16).astype(F32) * part
            hidden_grad = gate * part
            joint[:, n * 256 : n * 256 + 128] = (
                hidden_grad * up * s * (1.0 + gate_pre * (1.0 - s))
            ).astype(BF16)
            joint[:, n * 256 + 128 : n * 256 + 256] = (hidden_grad * active).astype(BF16)
            joint[:, 2 * H + n * 128 : 2 * H + n * 128 + 128] = (gate * hidden).astype(BF16)
            if n > 0:
                add_up(token_rows, n * 256 - 256, n * 256)
            if n % 2 == 0 and n > 0:
                add_up(grad_rows, 2 * H + n * 128 - 256, 2 * H + n * 128)
        add_up(token_rows, 2 * H - 256, 2 * H)
        add_up(grad_rows, 3 * H - 128, 3 * H)
        found = my_place == row
        gate_out[...] += jnp.sum(
            jnp.where(found, jnp.sum(dots, axis=1, keepdims=True), 0.0), axis=0, keepdims=True
        )

    back_send, back_recv = send.at[0], recv.at[0]

    def back_copy(k):
        return pltpu.make_async_remote_copy(
            src_ref=block(back_send, peer(k)),
            dst_ref=block(back_recv, e),
            send_sem=back_send_sem.at[k],
            recv_sem=back_recv_sem.at[k],
            device_id=(peer(k), d),
            device_id_type=MESH,
        )

    def send_back():
        own_joint = joint.at[pl.ds(pl.multiple_of(core * cap, 16), cap), :]
        for at in range(0, D, 256):
            own_rows[:, at : at + 256] = matmul_nt(
                own_joint[:, : 2 * H], w[at : at + 256, : 2 * H]
            ).astype(BF16)
        back_send[...] = matmul(pack[...], own_rows[...]).astype(BF16)

        @pl.loop(1, 16)
        def _(k):
            back_copy(k).start()

        back_recv[own, :] = back_send[own, :]

    def combine():
        @pl.loop(1, 16)
        def _(k):
            back_copy(k).wait_recv()

        token_out[...] = matmul_tn(sel[...], back_recv[...]).astype(BF16)

    gate_out[...] = jnp.zeros((1, 128), F32)
    acc[...] = jnp.zeros(acc.shape, F32)
    launch_next(0)
    enter(0)
    launch_next(1)
    enter(1)
    forward(0)

    @pl.loop(1, 8)
    def _(k):
        gate_copy(k).wait_recv()

    @pl.loop(0, TILES)
    def _(n):
        load_part(n, 0).wait()
        load_part(n, 1).wait()

    load_down.wait()
    to_other(0).wait_recv()
    to_other(1).wait_recv()

    @pl.loop(0, 8)
    def _(t):
        @pl.when(t == 1)
        def _():
            launch_next(2)
            enter(2)
            forward(1)
            left_to_other(0).wait_recv()
            left_to_other(1).wait_recv()

        @pl.when(t == 2)
        def _():
            enter(3)
            right_to_other(0).wait_recv()
            right_to_other(1).wait_recv()

        @pl.when(t == 3)
        def _():
            forward(2)
            forward_far(0)
            forward_far(1)
            to_other(2).wait_recv()
            to_other(3).wait_recv()

        @pl.when(t == 4)
        def _():
            send_back()
            far_to_other(0).wait_recv()
            far_to_other(1).wait_recv()

        @pl.when(t == 5)
        def _():
            forward(3)
            left_to_other(2).wait_recv()
            left_to_other(3).wait_recv()

        @pl.when(t == 6)
        def _():
            forward_far(2)
            right_to_other(2).wait_recv()
            right_to_other(3).wait_recv()

        @pl.when(t == 7)
        def _():
            forward_far(3)
            far_to_other(2).wait_recv()
            far_to_other(3).wait_recv()

        finishing = (t == 3) | (t >= 5)

        @pl.when(jnp.logical_not(finishing))
        def _():
            project(t - t // 4)

        @pl.when(finishing)
        def _():
            finish((t // 5) * (t - 4))

    combine()
    for n in range(TILES):
        for part in range(2):
            weight_out[:, part * H + n * 128 : part * H + n * 128 + 128] = acc[
                :, n * 256 + part * 128 : n * 256 + part * 128 + 128
            ].astype(BF16)
    weight_out[:, 2 * H :] = acc[:, 2 * H :].astype(BF16)

    @pl.loop(1, 16)
    def _(k):
        s1_copy(3, k).wait_send()

    for q in range(4):
        for copy in (
            to_right,
            to_left,
            to_other,
            onward,
            left_to_other,
            right_to_other,
            far_to_other,
        ):
            copy(q).wait_send()

    @pl.loop(1, 8)
    def _(k):
        gate_copy(k).wait_send()

    @pl.loop(1, 16)
    def _(k):
        back_copy(k).wait_send()


def layer(cap, picks, gates, tokens, grads, matrix):
    vmem = pl.BlockSpec(memory_space=pltpu.VMEM)
    dma = pltpu.SemaphoreType.DMA
    return pl.pallas_call(
        functools.partial(kernel, cap),
        name=f"moe_backward_{cap}",
        out_shape=(
            pltpu.VMEM((TOK, D), BF16),
            pltpu.VMEM((D // DP, 3 * H), BF16),
            jax.ShapeDtypeStruct((1, ROWS), F32),
            jax.ShapeDtypeStruct((1, 1), F32),
        ),
        in_specs=[vmem, vmem, vmem, vmem, pl.BlockSpec(memory_space=pl.ANY)],
        out_specs=(vmem, vmem, vmem, pl.BlockSpec(memory_space=pltpu.SMEM)),
        scratch_shapes=[
            pltpu.VMEM((D, 3 * H), BF16),
            pltpu.VMEM((2, SLOTS, D), BF16),
            pltpu.VMEM((2, SLOTS, D), BF16),
            pltpu.VMEM((2, 4, 2 * cap, D), BF16),
            pltpu.VMEM((3, 2 * cap, 2 * H), F32),
            pltpu.VMEM((2 * cap, 3 * H), BF16),
            pltpu.VMEM((D // DP, 3 * H), F32),
            pltpu.VMEM((SLOTS, TOK), BF16),
            pltpu.VMEM((SLOTS, cap), BF16),
            pltpu.VMEM((cap, D), BF16),
            pltpu.VMEM((EXPERTS * DP, ROWS), I32),
            pltpu.VMEM((1, 8 * ROWS), F32),
            pltpu.VMEM((8, 8, ROWS), F32),
            dma((2 * TILES + 1,)),
            dma((4, 16)),
            dma((4, 16)),
            dma((8,)),
            dma((8,)),
            dma((4, 7)),
            dma((4, 7)),
            dma((16,)),
            dma((16,)),
        ],
        compiler_params=pltpu.CompilerParams(
            collective_id=0, has_side_effects=True, vmem_limit_bytes=58 * 2**20
        ),
    )(picks, gates, tokens, grads, matrix)


def expert_pass(inputs, upstream, scales, matrix):
    hidden_width = matrix.shape[1] // 3
    gate_up = matrix[:, : 2 * hidden_width]
    down_proj = matrix[:, 2 * hidden_width :]
    projected = jnp.dot(inputs, gate_up, preferred_element_type=jnp.float32)
    gate_pre = projected[:, :hidden_width]
    up_values = projected[:, hidden_width:]
    logistic = jax.nn.sigmoid(gate_pre)
    activated = gate_pre * logistic
    hidden = (activated * up_values).astype(jnp.bfloat16)
    contract = (((1,), (1,)), ((), ()))
    output = lax.dot_general(hidden, down_proj, contract, preferred_element_type=jnp.float32)
    gate_grad = jnp.sum(upstream.astype(jnp.float32) * output, axis=1)
    scaled = (scales[:, None] * upstream.astype(jnp.float32)).astype(jnp.bfloat16)
    hidden_grad = jnp.dot(scaled, down_proj, preferred_element_type=jnp.float32)
    pre_grad = (hidden_grad * up_values * logistic * (1.0 + gate_pre * (1.0 - logistic))).astype(
        jnp.bfloat16
    )
    up_grad = (hidden_grad * activated).astype(jnp.bfloat16)
    joint_grad = jnp.concatenate([pre_grad, up_grad], axis=1)
    token_part = lax.dot_general(joint_grad, gate_up, contract, preferred_element_type=jnp.float32)
    return (token_part, gate_grad, joint_grad, hidden, scaled)


def any_load(tokens, out_grad, weights, gate_values, expert_picks):
    expert_count = lax.axis_size("expert")
    data_count = lax.axis_size("dp")
    holders = expert_count * data_count
    tok_rows = tokens.shape[0]
    width = tokens.shape[1]
    capacity = expert_picks.shape[1]
    rows = capacity // data_count
    slots = 2 * rows // holders
    total_slots = holders * slots
    expert_index = lax.axis_index("expert")
    data_index = lax.axis_index("dp")
    owner_index = expert_index * data_count + data_index
    contract_rows = (((0,), (0,)), ((), ()))
    sources = expert_picks // tok_rows
    held_here = (sources == owner_index).reshape(expert_picks.shape[0], data_count, rows)
    upto = jnp.arange(rows)[:, None] <= jnp.arange(rows)[None, :]
    ranks = matmul(held_here.astype(BF16), upto.astype(BF16)).astype(jnp.int32) - 1
    targets = (
        jnp.arange(expert_picks.shape[0], dtype=jnp.int32)[:, None, None] * data_count
        + jnp.arange(data_count, dtype=jnp.int32)[None, :, None]
    )
    positions = jnp.where(held_here, targets * slots + ranks, total_slots)
    local_rows = (expert_picks - owner_index * tok_rows).reshape(positions.shape)
    slot_table = (
        jnp.full((total_slots,), tok_rows, jnp.int32)
        .at[positions.reshape(-1)]
        .set(local_rows.reshape(-1), mode="drop")
    )
    zero_row = jnp.zeros((1, width), jnp.bfloat16)
    send_tokens = jnp.concatenate([tokens, zero_row], axis=0)[slot_table].reshape(
        holders, slots, width
    )
    send_grads = jnp.concatenate([out_grad, zero_row], axis=0)[slot_table].reshape(
        holders, slots, width
    )
    got_tokens, got_grads = (
        lax.all_to_all(send_tokens, ("expert", "dp"), split_axis=0, concat_axis=0, tiled=True),
        lax.all_to_all(send_grads, ("expert", "dp"), split_axis=0, concat_axis=0, tiled=True),
    )
    flat_tokens = got_tokens.reshape(total_slots, width)
    flat_grads = got_grads.reshape(total_slots, width)
    own_picks = lax.dynamic_slice(expert_picks, (expert_index, data_index * rows), (1, rows))[0]
    pick_sources = own_picks // tok_rows
    steps_index = jnp.arange(rows, dtype=jnp.int32)
    earlier = steps_index[:, None] > steps_index[None, :]
    same_source = pick_sources[:, None] == pick_sources[None, :]
    pick_ranks = jnp.sum((earlier & same_source).astype(jnp.int32), axis=1)
    pick_slots = pick_sources * slots + pick_ranks
    scales = gate_values[0]
    matrix = weights[0]
    inputs = flat_tokens[pick_slots]
    upstream = flat_grads[pick_slots]
    token_part, gate_grad, joint_grad, hidden, scaled = expert_pass(
        inputs, upstream, scales, matrix
    )
    back_rows = jnp.zeros((total_slots, width), jnp.float32).at[pick_slots].set(token_part)
    left_part = lax.dot_general(
        inputs, joint_grad, contract_rows, preferred_element_type=jnp.float32
    )
    right_part = lax.dot_general(scaled, hidden, contract_rows, preferred_element_type=jnp.float32)
    parts = jnp.concatenate([left_part, right_part], axis=1).reshape(data_count, -1, 3 * H)
    summed = jnp.sum(lax.all_to_all(parts, "dp", split_axis=0, concat_axis=0, tiled=True), axis=0)
    weight_grad = summed.astype(jnp.bfloat16)[None]
    returned = lax.all_to_all(
        back_rows.reshape(holders, slots, width),
        ("expert", "dp"),
        split_axis=0,
        concat_axis=0,
        tiled=True,
    )
    token_sum = (
        jnp.zeros((tok_rows + 1, width), jnp.float32)
        .at[slot_table]
        .add(returned.reshape(total_slots, width))
    )
    token_grad = token_sum[:tok_rows].astype(jnp.bfloat16)
    return (token_grad, weight_grad, gate_grad[None])


def copy_kernel(token_in, weight_in, gate_in, token_out, weight_out, gate_out, sems):
    moves = [
        pltpu.make_async_copy(token_in, token_out, sems.at[0]),
        pltpu.make_async_copy(weight_in, weight_out, sems.at[1]),
        pltpu.make_async_copy(gate_in, gate_out, sems.at[2]),
    ]
    for move in moves:
        move.start()
    for move in moves:
        move.wait()


def hand_over(*made):
    return tuple(
        pl.pallas_call(
            copy_kernel,
            name="hand_over",
            out_shape=[jax.ShapeDtypeStruct(m.shape, m.dtype) for m in made],
            in_specs=[pl.BlockSpec(memory_space=pltpu.VMEM)] * 3,
            out_specs=[pl.BlockSpec(memory_space=pl.ANY)] * 3,
            scratch_shapes=[pltpu.SemaphoreType.DMA((3,))],
            compiler_params=pltpu.CompilerParams(vmem_limit_bytes=60 * 2**20),
        )(*made)
    )


CAP = 160


def shards(tokens, out_grad, weights, gate_values, expert_picks):
    *made, most = layer(CAP, expert_picks, gate_values, tokens, out_grad, weights[0])
    given = (tokens, out_grad, weights, gate_values, expert_picks)

    def otherwise(made, given):
        token_grad, weight_grad, gate_grad = any_load(*given)
        return token_grad, weight_grad[0], gate_grad

    token_grad, weight_grad, gate_grad = lax.cond(
        most[0, 0] <= CAP, lambda made, given: hand_over(*made), otherwise, made, given
    )
    return token_grad, weight_grad[None], gate_grad


def solution(mesh):
    return jax.shard_map(
        shards,
        mesh=mesh,
        in_specs=(
            P(("expert", "dp"), None),
            P(("expert", "dp"), None),
            P("expert", None, None),
            P("expert", "dp"),
            P(),
        ),
        out_specs=(P(("expert", "dp"), None), P("expert", "dp", None), P("expert", "dp")),
        check_vma=False,
    )
```

```python
import functools

import jax
import jax.numpy as jnp
from jax import lax
from jax.experimental import pallas as pl
from jax.experimental.pallas import tpu as pltpu
from jax.sharding import PartitionSpec as P

MESH = pl.DeviceIdType.MESH
F32 = jnp.float32
BF16 = jnp.bfloat16
I32 = jnp.int32
D = 2048
H = 1408
EXPERTS = 16
DP = 8
TOK = 256
SLOTS = 256
ROWS = 128
TILES = H // 128
HALF = D // 2


def iota(shape, axis):
    return lax.broadcasted_iota(I32, shape, axis)


def matmul(a, b):
    return jnp.dot(a, b, preferred_element_type=F32)


def matmul_tn(a, b):
    return lax.dot_general(a, b, (((0,), (0,)), ((), ())), preferred_element_type=F32)


def matmul_nt(a, b):
    return lax.dot_general(a, b, (((1,), (1,)), ((), ())), preferred_element_type=F32)


def slot_column(mask, values, tri):
    ones = jnp.where(mask, 1.0, 0.0)
    rank = matmul(ones.astype(BF16), tri) * ones
    rank3 = rank.reshape(16, 8, 128)
    value3 = values.reshape(16, 8, 128)
    ranks = jnp.concatenate([rank3, rank3], axis=1).reshape(SLOTS, 128)
    twice = jnp.concatenate([value3, value3], axis=1).reshape(SLOTS, 128)
    wanted = ((iota((SLOTS, 128), 0) // 8) % 2 + 1).astype(F32)
    return jnp.sum(jnp.where(ranks == wanted, twice + 1.0, 0.0), axis=1, keepdims=True) - 1.0


def kernel(
    cap,
    all_picks_ref,
    gates_ref,
    tok_ref,
    grad_ref,
    w_hbm,
    token_out,
    weight_out,
    gate_out,
    most_out,
    w,
    send,
    recv,
    gathered,
    gate_up,
    joint,
    acc,
    sel,
    pack,
    own_rows,
    picks_ref,
    place,
    all_gates,
    w_sem,
    s1_send,
    s1_recv,
    gate_send,
    gate_recv,
    ring_send,
    ring_recv,
    back_send_sem,
    back_recv_sem,
):
    e = lax.axis_index("expert")
    d = lax.axis_index("dp")
    ey, ez = e // 4, e % 4
    x, core = d // 2, d % 2
    me = e * DP + d
    right = ((x + 1) % 4) * 2 + core
    left = ((x + 3) % 4) * 2 + core
    other = x * 2 + 1 - core

    def load_part(n, half):
        return pltpu.make_async_copy(
            w_hbm.at[:, pl.ds(pl.multiple_of(half * H + n * 128, 128), 128)],
            w.at[:, pl.ds(pl.multiple_of(n * 256 + half * 128, 128), 128)],
            w_sem.at[n * 2 + half],
        )

    load_down = pltpu.make_async_copy(
        w_hbm.at[:, 2 * H : 3 * H], w.at[:, 2 * H : 3 * H], w_sem.at[2 * TILES]
    )

    @pl.loop(0, TILES)
    def _(n):
        load_part(n, 0).start()
        load_part(n, 1).start()

    load_down.start()

    def peer(k):
        return ((ey + k // 4) % 4) * 4 + (ez + k % 4) % 4

    barrier = pltpu.get_barrier_semaphore()

    @pl.loop(1, 16)
    def _(k):
        pl.semaphore_signal(barrier, inc=1, device_id=(peer(k), d), device_id_type=MESH)

    @pl.loop(1, 8)
    def _(k):
        pl.semaphore_signal(barrier, inc=1, device_id=(e, (d + k) % 8), device_id_type=MESH)

    tri = jnp.where(iota((128, 128), 0) <= iota((128, 128), 1), 1.0, 0.0).astype(BF16)
    picks_ref[...] = all_picks_ref[...].reshape(EXPERTS * DP, ROWS)
    picks = picks_ref[...]
    token_of = slot_column((picks >> 8) == me, (picks & 255).astype(F32), tri)
    sel[...] = jnp.where(token_of == iota((SLOTS, TOK), 1).astype(F32), 1.0, 0.0).astype(BF16)
    all_gates[d] = jnp.broadcast_to(gates_ref[...], (8, 128))

    def block(ref, row):
        return ref.at[pl.ds(pl.multiple_of(row * 16, 16), 16), :]

    def columns(q):
        return slice((q % 2) * HALF, (q % 2) * HALF + HALF)

    def s1_copy(q, k):
        return pltpu.make_async_remote_copy(
            src_ref=block(send.at[q // 2], peer(k)).at[:, columns(q)],
            dst_ref=block(recv.at[q // 2], e).at[:, columns(q)],
            send_sem=s1_send.at[q, k],
            recv_sem=s1_recv.at[q, k],
            device_id=(peer(k), d),
            device_id_type=MESH,
        )

    def gate_copy(k):
        return pltpu.make_async_remote_copy(
            src_ref=all_gates.at[d],
            dst_ref=all_gates.at[d],
            send_sem=gate_send.at[k],
            recv_sem=gate_recv.at[k],
            device_id=(e, (d + k) % 8),
            device_id_type=MESH,
        )

    def launch(q):
        @pl.loop(1, 16)
        def _(k):
            s1_copy(q, k).start()

    def launch_next(q):
        @pl.loop(1, 16)
        def _(k):
            s1_copy(q, k).wait_send()

        launch(q + 1)

    own = pl.ds(pl.multiple_of(e * 16, 16), 16)
    for q in range(4):
        ref = (tok_ref, grad_ref)[q // 2]
        send[q // 2, :, columns(q)] = matmul(sel[...], ref[:, columns(q)]).astype(BF16)
        if q == 0:
            pl.semaphore_wait(barrier, 22)
            launch(0)
        recv[q // 2, own, columns(q)] = send[q // 2, own, columns(q)]

    @pl.loop(1, 8)
    def _(k):
        gate_copy(k).start()

    mine = picks_ref[pl.ds(pl.multiple_of(e * 8, 8), 8), :]
    sources = mine >> 8
    planes = sources & 7
    before = jnp.zeros((8, 1), F32)
    positions = []
    for b in range(8):
        hit = jnp.where(
            jnp.broadcast_to(planes[b : b + 1, :], (8, 128)) == iota((8, 128), 0), 1.0, 0.0
        )
        count = matmul(hit.astype(BF16), tri)
        positions.append(jnp.sum(hit * (count + before), axis=0, keepdims=True) - 1.0)
        before = before + count[:, 127:128]
    position = jnp.concatenate(positions, axis=0)
    rows_of = position + planes.astype(F32) * cap
    for b in range(8):
        place[:, b * 128 : (b + 1) * 128] = rows_of[b : b + 1, :]
    holders = iota((16, 8, 128), 0) * DP + d
    held = (jnp.broadcast_to(sources[None], (16, 8, 128)) == holders).reshape(128, 128)
    packed_at = slot_column(
        held, jnp.broadcast_to(position[None], (16, 8, 128)).reshape(128, 128), tri
    )
    pack[...] = jnp.where(packed_at == iota((SLOTS, cap), 1).astype(F32), 1.0, 0.0).astype(BF16)

    most = jnp.zeros((16, 1), F32)
    planes_of = (picks >> 8) & 7
    for plane in range(8):
        counts = jnp.sum(jnp.where(planes_of == plane, 1.0, 0.0), axis=1, keepdims=True)
        most = jnp.maximum(most, jnp.sum(counts.reshape(16, 8, 1), axis=1))
    most_out[0, 0] = jnp.max(most)

    lx, rx, ox = (x + 3) % 4, (x + 1) % 4, (x + 2) % 4

    def ring(q, kind, chip, to):
        rows = pl.ds(pl.multiple_of(core * cap, 16), cap)
        part = gathered.at[q // 2, chip, rows, columns(q)]
        return pltpu.make_async_remote_copy(
            src_ref=part,
            dst_ref=part,
            send_sem=ring_send.at[q, kind],
            recv_sem=ring_recv.at[q, kind],
            device_id=(e, to),
            device_id_type=MESH,
        )

    def to_right(q):
        return ring(q, 0, x, right)

    def to_left(q):
        return ring(q, 1, x, left)

    def to_other(q):
        return ring(q, 2, x, other)

    def onward(q):
        return ring(q, 3, lx, right) if q % 2 == 0 else ring(q, 3, rx, left)

    def left_to_other(q):
        return ring(q, 4, lx, other)

    def right_to_other(q):
        return ring(q, 5, rx, other)

    def far_to_other(q):
        return ring(q, 6, ox, other)

    def enter(q):
        @pl.loop(1, 16)
        def _(k):
            s1_copy(q, k).wait_recv()

        rows = pl.ds(pl.multiple_of(core * cap, 16), cap)
        gathered[q // 2, x, rows, columns(q)] = matmul_tn(
            pack[...], recv[q // 2, :, columns(q)]
        ).astype(BF16)
        to_right(q).start()
        to_left(q).start()
        to_other(q).start()

    def forward(q):
        to_right(q).wait_recv()
        to_left(q).wait_recv()
        onward(q).start()
        left_to_other(q).start()
        right_to_other(q).start()

    def forward_far(q):
        onward(q).wait_recv()
        far_to_other(q).start()

    slice_d = pl.ds(pl.multiple_of(d * 256, 256), 256)
    my_place = place[:, pl.ds(pl.multiple_of(d * 128, 128), 128)]

    def chip_at(j):
        hop = (j + 1) // 2
        return (x + hop + (j % 2) * (4 - 2 * hop)) % 4

    def project(j):
        chip, slot = chip_at(j), j % 3
        for n in range(TILES):
            gate_up[slot, :, n * 256 : n * 256 + 256] = matmul(
                gathered[0, chip], w[:, n * 256 : n * 256 + 256]
            )

    def finish(j):
        chip, slot = chip_at(j), j % 3
        row = (chip * 2 * cap + iota((2 * cap, 1), 0)).astype(F32)
        gate_row = jnp.concatenate([all_gates[b, 0:1, :] for b in range(8)], axis=1)
        gate = jnp.sum(jnp.where(place[...] == row, gate_row, 0.0), axis=1, keepdims=True)
        dots = jnp.zeros((2 * cap, 128), F32)
        token_rows = gathered[0, chip, :, slice_d].T
        grad_rows = gathered[1, chip, :, slice_d].T

        def upstream(n):
            low = 2 * H + n * 256
            return matmul(gathered[1, chip], w[:, low : min(low + 256, 3 * H)])

        def add_up(rows, low, high):
            acc[:, low:high] += matmul(rows, joint[:, low:high])

        following = upstream(0)
        for n in range(TILES):
            if n % 2 == 0:
                u = following
                if n // 2 + 1 < (TILES + 1) // 2:
                    following = upstream(n // 2 + 1)
            part = u[:, (n % 2) * 128 : (n % 2) * 128 + 128]
            gate_pre = gate_up[slot, :, n * 256 : n * 256 + 128]
            up = gate_up[slot, :, n * 256 + 128 : n * 256 + 256]
            s = 0.5 + 0.5 * jnp.tanh(0.5 * gate_pre)
            active = gate_pre * s
            hidden = active * up
            dots += hidden.astype(BF16).astype(F32) * part
            hidden_grad = gate * part
            joint[:, n * 256 : n * 256 + 128] = (
                hidden_grad * up * (s + active * (1.0 - s))
            ).astype(BF16)
            joint[:, n * 256 + 128 : n * 256 + 256] = (hidden_grad * active).astype(BF16)
            joint[:, 2 * H + n * 128 : 2 * H + n * 128 + 128] = (gate * hidden).astype(BF16)
            if n > 0:
                add_up(token_rows, n * 256 - 256, n * 256)
            if n % 2 == 0 and n > 0:
                add_up(grad_rows, 2 * H + n * 128 - 256, 2 * H + n * 128)
        add_up(token_rows, 2 * H - 256, 2 * H)
        add_up(grad_rows, 3 * H - 128, 3 * H)
        found = my_place == row
        gate_out[...] += jnp.sum(
            jnp.where(found, jnp.sum(dots, axis=1, keepdims=True), 0.0), axis=0, keepdims=True
        )

    back_send, back_recv = send.at[0], recv.at[0]

    def back_copy(k):
        return pltpu.make_async_remote_copy(
            src_ref=block(back_send, peer(k)),
            dst_ref=block(back_recv, e),
            send_sem=back_send_sem.at[k],
            recv_sem=back_recv_sem.at[k],
            device_id=(peer(k), d),
            device_id_type=MESH,
        )

    def send_back():
        own_joint = joint.at[pl.ds(pl.multiple_of(core * cap, 16), cap), :]
        for at in range(0, D, 256):
            own_rows[:, at : at + 256] = matmul_nt(
                own_joint[:, : 2 * H], w[at : at + 256, : 2 * H]
            ).astype(BF16)
        back_send[...] = matmul(pack[...], own_rows[...]).astype(BF16)

        @pl.loop(1, 16)
        def _(k):
            back_copy(k).start()

        back_recv[own, :] = back_send[own, :]

    def combine():
        @pl.loop(1, 16)
        def _(k):
            back_copy(k).wait_recv()

        token_out[...] = matmul_tn(sel[...], back_recv[...]).astype(BF16)

    gate_out[...] = jnp.zeros((1, 128), F32)
    acc[...] = jnp.zeros(acc.shape, F32)
    launch_next(0)
    enter(0)
    launch_next(1)
    enter(1)
    forward(0)

    @pl.loop(1, 8)
    def _(k):
        gate_copy(k).wait_recv()

    @pl.loop(0, TILES)
    def _(n):
        load_part(n, 0).wait()
        load_part(n, 1).wait()

    load_down.wait()
    to_other(0).wait_recv()
    to_other(1).wait_recv()

    @pl.loop(0, 8)
    def _(t):
        @pl.when(t == 1)
        def _():
            launch_next(2)
            enter(2)
            forward(1)
            left_to_other(0).wait_recv()
            left_to_other(1).wait_recv()

        @pl.when(t == 2)
        def _():
            enter(3)
            to_other(2).wait_recv()
            to_other(3).wait_recv()

        @pl.when(t == 3)
        def _():
            forward(2)
            right_to_other(0).wait_recv()
            right_to_other(1).wait_recv()

        @pl.when(t == 4)
        def _():
            forward_far(0)
            send_back()
            forward_far(1)
            forward(3)
            far_to_other(0).wait_recv()
            far_to_other(1).wait_recv()

        @pl.when(t == 5)
        def _():
            left_to_other(2).wait_recv()
            left_to_other(3).wait_recv()

        @pl.when(t == 6)
        def _():
            forward_far(2)
            right_to_other(2).wait_recv()
            right_to_other(3).wait_recv()

        @pl.when(t == 7)
        def _():
            forward_far(3)
            combine()
            far_to_other(2).wait_recv()
            far_to_other(3).wait_recv()

        finishing = (t == 2) | (t >= 5)

        @pl.when(jnp.logical_not(finishing))
        def _():
            project(t - t // 3)

        @pl.when(finishing)
        def _():
            finish((t // 5) * (t - 4))

    for n in range(TILES):
        for part in range(2):
            weight_out[:, part * H + n * 128 : part * H + n * 128 + 128] = acc[
                :, n * 256 + part * 128 : n * 256 + part * 128 + 128
            ].astype(BF16)
    weight_out[:, 2 * H :] = acc[:, 2 * H :].astype(BF16)

    @pl.loop(1, 16)
    def _(k):
        s1_copy(3, k).wait_send()

    for q in range(4):
        for copy in (
            to_right,
            to_left,
            to_other,
            onward,
            left_to_other,
            right_to_other,
            far_to_other,
        ):
            copy(q).wait_send()

    @pl.loop(1, 8)
    def _(k):
        gate_copy(k).wait_send()

    @pl.loop(1, 16)
    def _(k):
        back_copy(k).wait_send()


def layer(cap, picks, gates, tokens, grads, matrix):
    vmem = pl.BlockSpec(memory_space=pltpu.VMEM)
    dma = pltpu.SemaphoreType.DMA
    return pl.pallas_call(
        functools.partial(kernel, cap),
        name=f"moe_backward_{cap}",
        out_shape=(
            pltpu.VMEM((TOK, D), BF16),
            pltpu.VMEM((D // DP, 3 * H), BF16),
            jax.ShapeDtypeStruct((1, ROWS), F32),
            jax.ShapeDtypeStruct((1, 1), F32),
        ),
        in_specs=[vmem, vmem, vmem, vmem, pl.BlockSpec(memory_space=pl.ANY)],
        out_specs=(vmem, vmem, vmem, pl.BlockSpec(memory_space=pltpu.SMEM)),
        scratch_shapes=[
            pltpu.VMEM((D, 3 * H), BF16),
            pltpu.VMEM((2, SLOTS, D), BF16),
            pltpu.VMEM((2, SLOTS, D), BF16),
            pltpu.VMEM((2, 4, 2 * cap, D), BF16),
            pltpu.VMEM((3, 2 * cap, 2 * H), F32),
            pltpu.VMEM((2 * cap, 3 * H), BF16),
            pltpu.VMEM((D // DP, 3 * H), F32),
            pltpu.VMEM((SLOTS, TOK), BF16),
            pltpu.VMEM((SLOTS, cap), BF16),
            pltpu.VMEM((cap, D), BF16),
            pltpu.VMEM((EXPERTS * DP, ROWS), I32),
            pltpu.VMEM((1, 8 * ROWS), F32),
            pltpu.VMEM((8, 8, ROWS), F32),
            dma((2 * TILES + 1,)),
            dma((4, 16)),
            dma((4, 16)),
            dma((8,)),
            dma((8,)),
            dma((4, 7)),
            dma((4, 7)),
            dma((16,)),
            dma((16,)),
        ],
        compiler_params=pltpu.CompilerParams(
            collective_id=0, has_side_effects=True, vmem_limit_bytes=58 * 2**20
        ),
    )(picks, gates, tokens, grads, matrix)


def expert_pass(inputs, upstream, scales, matrix):
    hidden_width = matrix.shape[1] // 3
    gate_up = matrix[:, : 2 * hidden_width]
    down_proj = matrix[:, 2 * hidden_width :]
    projected = jnp.dot(inputs, gate_up, preferred_element_type=jnp.float32)
    gate_pre = projected[:, :hidden_width]
    up_values = projected[:, hidden_width:]
    logistic = jax.nn.sigmoid(gate_pre)
    activated = gate_pre * logistic
    hidden = (activated * up_values).astype(jnp.bfloat16)
    contract = (((1,), (1,)), ((), ()))
    output = lax.dot_general(hidden, down_proj, contract, preferred_element_type=jnp.float32)
    gate_grad = jnp.sum(upstream.astype(jnp.float32) * output, axis=1)
    scaled = (scales[:, None] * upstream.astype(jnp.float32)).astype(jnp.bfloat16)
    hidden_grad = jnp.dot(scaled, down_proj, preferred_element_type=jnp.float32)
    pre_grad = (hidden_grad * up_values * logistic * (1.0 + gate_pre * (1.0 - logistic))).astype(
        jnp.bfloat16
    )
    up_grad = (hidden_grad * activated).astype(jnp.bfloat16)
    joint_grad = jnp.concatenate([pre_grad, up_grad], axis=1)
    token_part = lax.dot_general(joint_grad, gate_up, contract, preferred_element_type=jnp.float32)
    return (token_part, gate_grad, joint_grad, hidden, scaled)


def any_load(tokens, out_grad, weights, gate_values, expert_picks):
    expert_count = lax.axis_size("expert")
    data_count = lax.axis_size("dp")
    holders = expert_count * data_count
    tok_rows = tokens.shape[0]
    width = tokens.shape[1]
    capacity = expert_picks.shape[1]
    rows = capacity // data_count
    slots = 2 * rows // holders
    total_slots = holders * slots
    expert_index = lax.axis_index("expert")
    data_index = lax.axis_index("dp")
    owner_index = expert_index * data_count + data_index
    contract_rows = (((0,), (0,)), ((), ()))
    sources = expert_picks // tok_rows
    held_here = (sources == owner_index).reshape(expert_picks.shape[0], data_count, rows)
    upto = jnp.arange(rows)[:, None] <= jnp.arange(rows)[None, :]
    ranks = matmul(held_here.astype(BF16), upto.astype(BF16)).astype(jnp.int32) - 1
    targets = (
        jnp.arange(expert_picks.shape[0], dtype=jnp.int32)[:, None, None] * data_count
        + jnp.arange(data_count, dtype=jnp.int32)[None, :, None]
    )
    positions = jnp.where(held_here, targets * slots + ranks, total_slots)
    local_rows = (expert_picks - owner_index * tok_rows).reshape(positions.shape)
    slot_table = (
        jnp.full((total_slots,), tok_rows, jnp.int32)
        .at[positions.reshape(-1)]
        .set(local_rows.reshape(-1), mode="drop")
    )
    zero_row = jnp.zeros((1, width), jnp.bfloat16)
    send_tokens = jnp.concatenate([tokens, zero_row], axis=0)[slot_table].reshape(
        holders, slots, width
    )
    send_grads = jnp.concatenate([out_grad, zero_row], axis=0)[slot_table].reshape(
        holders, slots, width
    )
    got_tokens, got_grads = (
        lax.all_to_all(send_tokens, ("expert", "dp"), split_axis=0, concat_axis=0, tiled=True),
        lax.all_to_all(send_grads, ("expert", "dp"), split_axis=0, concat_axis=0, tiled=True),
    )
    flat_tokens = got_tokens.reshape(total_slots, width)
    flat_grads = got_grads.reshape(total_slots, width)
    own_picks = lax.dynamic_slice(expert_picks, (expert_index, data_index * rows), (1, rows))[0]
    pick_sources = own_picks // tok_rows
    steps_index = jnp.arange(rows, dtype=jnp.int32)
    earlier = steps_index[:, None] > steps_index[None, :]
    same_source = pick_sources[:, None] == pick_sources[None, :]
    pick_ranks = jnp.sum((earlier & same_source).astype(jnp.int32), axis=1)
    pick_slots = pick_sources * slots + pick_ranks
    scales = gate_values[0]
    matrix = weights[0]
    inputs = flat_tokens[pick_slots]
    upstream = flat_grads[pick_slots]
    token_part, gate_grad, joint_grad, hidden, scaled = expert_pass(
        inputs, upstream, scales, matrix
    )
    back_rows = jnp.zeros((total_slots, width), jnp.float32).at[pick_slots].set(token_part)
    left_part = lax.dot_general(
        inputs, joint_grad, contract_rows, preferred_element_type=jnp.float32
    )
    right_part = lax.dot_general(scaled, hidden, contract_rows, preferred_element_type=jnp.float32)
    parts = jnp.concatenate([left_part, right_part], axis=1).reshape(data_count, -1, 3 * H)
    summed = jnp.sum(lax.all_to_all(parts, "dp", split_axis=0, concat_axis=0, tiled=True), axis=0)
    weight_grad = summed.astype(jnp.bfloat16)[None]
    returned = lax.all_to_all(
        back_rows.reshape(holders, slots, width),
        ("expert", "dp"),
        split_axis=0,
        concat_axis=0,
        tiled=True,
    )
    token_sum = (
        jnp.zeros((tok_rows + 1, width), jnp.float32)
        .at[slot_table]
        .add(returned.reshape(total_slots, width))
    )
    token_grad = token_sum[:tok_rows].astype(jnp.bfloat16)
    return (token_grad, weight_grad, gate_grad[None])


def copy_kernel(token_in, weight_in, gate_in, token_out, weight_out, gate_out, sems):
    moves = [
        pltpu.make_async_copy(token_in, token_out, sems.at[0]),
        pltpu.make_async_copy(weight_in, weight_out, sems.at[1]),
        pltpu.make_async_copy(gate_in, gate_out, sems.at[2]),
    ]
    for move in moves:
        move.start()
    for move in moves:
        move.wait()


def hand_over(*made):
    return tuple(
        pl.pallas_call(
            copy_kernel,
            name="hand_over",
            out_shape=[jax.ShapeDtypeStruct(m.shape, m.dtype) for m in made],
            in_specs=[pl.BlockSpec(memory_space=pltpu.VMEM)] * 3,
            out_specs=[pl.BlockSpec(memory_space=pl.ANY)] * 3,
            scratch_shapes=[pltpu.SemaphoreType.DMA((3,))],
            compiler_params=pltpu.CompilerParams(vmem_limit_bytes=60 * 2**20),
        )(*made)
    )


CAP = 160


def shards(tokens, out_grad, weights, gate_values, expert_picks):
    *made, most = layer(CAP, expert_picks, gate_values, tokens, out_grad, weights[0])
    given = (tokens, out_grad, weights, gate_values, expert_picks)

    def otherwise(made, given):
        token_grad, weight_grad, gate_grad = any_load(*given)
        return token_grad, weight_grad[0], gate_grad

    token_grad, weight_grad, gate_grad = lax.cond(
        most[0, 0] <= CAP, lambda made, given: hand_over(*made), otherwise, made, given
    )
    return token_grad, weight_grad[None], gate_grad


def solution(mesh):
    return jax.shard_map(
        shards,
        mesh=mesh,
        in_specs=(
            P(("expert", "dp"), None),
            P(("expert", "dp"), None),
            P("expert", None, None),
            P("expert", "dp"),
            P(),
        ),
        out_specs=(P(("expert", "dp"), None), P("expert", "dp", None), P("expert", "dp")),
        check_vma=False,
    )
```

```python
import functools

import jax
import jax.numpy as jnp
from jax import lax
from jax.experimental import pallas as pl
from jax.experimental.pallas import tpu as pltpu
from jax.sharding import PartitionSpec as P

MESH = pl.DeviceIdType.MESH
F32 = jnp.float32
BF16 = jnp.bfloat16
I32 = jnp.int32
D = 2048
H = 1408
EXPERTS = 16
DP = 8
TOK = 256
SLOTS = 256
ROWS = 128
TILES = H // 128
HALF = D // 2


def iota(shape, axis):
    return lax.broadcasted_iota(I32, shape, axis)


def matmul(a, b):
    return jnp.dot(a, b, preferred_element_type=F32)


def matmul_tn(a, b):
    return lax.dot_general(a, b, (((0,), (0,)), ((), ())), preferred_element_type=F32)


def matmul_nt(a, b):
    return lax.dot_general(a, b, (((1,), (1,)), ((), ())), preferred_element_type=F32)


def slot_column(mask, values, tri):
    ones = jnp.where(mask, 1.0, 0.0)
    rank = matmul(ones.astype(BF16), tri) * ones
    rank3 = rank.reshape(16, 8, 128)
    value3 = values.reshape(16, 8, 128)
    ranks = jnp.concatenate([rank3, rank3], axis=1).reshape(SLOTS, 128)
    twice = jnp.concatenate([value3, value3], axis=1).reshape(SLOTS, 128)
    wanted = ((iota((SLOTS, 128), 0) // 8) % 2 + 1).astype(F32)
    return jnp.sum(jnp.where(ranks == wanted, twice + 1.0, 0.0), axis=1, keepdims=True) - 1.0


def kernel(
    cap,
    all_picks_ref,
    gates_ref,
    tok_ref,
    grad_ref,
    w_hbm,
    token_out,
    weight_out,
    gate_out,
    most_out,
    w,
    send,
    recv,
    gathered,
    gate_up,
    joint,
    acc,
    sel,
    pack,
    own_rows,
    picks_ref,
    place,
    all_gates,
    w_sem,
    s1_send,
    s1_recv,
    gate_send,
    gate_recv,
    ring_send,
    ring_recv,
    back_send_sem,
    back_recv_sem,
):
    e = lax.axis_index("expert")
    d = lax.axis_index("dp")
    ey, ez = e // 4, e % 4
    x, core = d // 2, d % 2
    me = e * DP + d
    right = ((x + 1) % 4) * 2 + core
    left = ((x + 3) % 4) * 2 + core
    other = x * 2 + 1 - core

    def load_part(n, half):
        return pltpu.make_async_copy(
            w_hbm.at[:, pl.ds(pl.multiple_of(half * H + n * 128, 128), 128)],
            w.at[:, pl.ds(pl.multiple_of(n * 256 + half * 128, 128), 128)],
            w_sem.at[n * 2 + half],
        )

    load_down = pltpu.make_async_copy(
        w_hbm.at[:, 2 * H : 3 * H], w.at[:, 2 * H : 3 * H], w_sem.at[2 * TILES]
    )

    @pl.loop(0, TILES)
    def _(n):
        load_part(n, 0).start()
        load_part(n, 1).start()

    load_down.start()

    def peer(k):
        return ((ey + k // 4) % 4) * 4 + (ez + k % 4) % 4

    barrier = pltpu.get_barrier_semaphore()

    @pl.loop(1, 16)
    def _(k):
        pl.semaphore_signal(barrier, inc=1, device_id=(peer(k), d), device_id_type=MESH)

    @pl.loop(1, 8)
    def _(k):
        pl.semaphore_signal(barrier, inc=1, device_id=(e, (d + k) % 8), device_id_type=MESH)

    tri = jnp.where(iota((128, 128), 0) <= iota((128, 128), 1), 1.0, 0.0).astype(BF16)
    picks_ref[...] = all_picks_ref[...].reshape(EXPERTS * DP, ROWS)
    picks = picks_ref[...]
    token_of = slot_column((picks >> 8) == me, (picks & 255).astype(F32), tri)
    sel[...] = jnp.where(token_of == iota((SLOTS, TOK), 1).astype(F32), 1.0, 0.0).astype(BF16)
    all_gates[d] = jnp.broadcast_to(gates_ref[...], (8, 128))

    def block(ref, row):
        return ref.at[pl.ds(pl.multiple_of(row * 16, 16), 16), :]

    def columns(q):
        return slice((q % 2) * HALF, (q % 2) * HALF + HALF)

    def s1_copy(q, k):
        return pltpu.make_async_remote_copy(
            src_ref=block(send.at[q // 2], peer(k)).at[:, columns(q)],
            dst_ref=block(recv.at[q // 2], e).at[:, columns(q)],
            send_sem=s1_send.at[q, k],
            recv_sem=s1_recv.at[q, k],
            device_id=(peer(k), d),
            device_id_type=MESH,
        )

    def gate_copy(k):
        return pltpu.make_async_remote_copy(
            src_ref=all_gates.at[d],
            dst_ref=all_gates.at[d],
            send_sem=gate_send.at[k],
            recv_sem=gate_recv.at[k],
            device_id=(e, (d + k) % 8),
            device_id_type=MESH,
        )

    def launch(q):
        @pl.loop(1, 16)
        def _(k):
            s1_copy(q, k).start()

    def launch_next(q):
        @pl.loop(1, 16)
        def _(k):
            s1_copy(q, k).wait_send()

        launch(q + 1)

    own = pl.ds(pl.multiple_of(e * 16, 16), 16)
    for q in range(4):
        ref = (tok_ref, grad_ref)[q // 2]
        send[q // 2, :, columns(q)] = matmul(sel[...], ref[:, columns(q)]).astype(BF16)
        if q == 0:
            pl.semaphore_wait(barrier, 22)
            launch(0)
        recv[q // 2, own, columns(q)] = send[q // 2, own, columns(q)]

    @pl.loop(1, 8)
    def _(k):
        gate_copy(k).start()

    mine = picks_ref[pl.ds(pl.multiple_of(e * 8, 8), 8), :]
    sources = mine >> 8
    planes = sources & 7
    before = jnp.zeros((8, 1), F32)
    positions = []
    for b in range(8):
        hit = jnp.where(
            jnp.broadcast_to(planes[b : b + 1, :], (8, 128)) == iota((8, 128), 0), 1.0, 0.0
        )
        count = matmul(hit.astype(BF16), tri)
        positions.append(jnp.sum(hit * (count + before), axis=0, keepdims=True) - 1.0)
        before = before + count[:, 127:128]
    position = jnp.concatenate(positions, axis=0)
    rows_of = position + planes.astype(F32) * cap
    for b in range(8):
        place[:, b * 128 : (b + 1) * 128] = rows_of[b : b + 1, :]
    holders = iota((16, 8, 128), 0) * DP + d
    held = (jnp.broadcast_to(sources[None], (16, 8, 128)) == holders).reshape(128, 128)
    packed_at = slot_column(
        held, jnp.broadcast_to(position[None], (16, 8, 128)).reshape(128, 128), tri
    )
    pack[...] = jnp.where(packed_at == iota((SLOTS, cap), 1).astype(F32), 1.0, 0.0).astype(BF16)

    most = jnp.zeros((16, 1), F32)
    planes_of = (picks >> 8) & 7
    for plane in range(8):
        counts = jnp.sum(jnp.where(planes_of == plane, 1.0, 0.0), axis=1, keepdims=True)
        most = jnp.maximum(most, jnp.sum(counts.reshape(16, 8, 1), axis=1))
    most_out[0, 0] = jnp.max(most)

    lx, rx, ox = (x + 3) % 4, (x + 1) % 4, (x + 2) % 4

    def ring(q, kind, chip, to):
        rows = pl.ds(pl.multiple_of(core * cap, 16), cap)
        part = gathered.at[q // 2, chip, rows, columns(q)]
        return pltpu.make_async_remote_copy(
            src_ref=part,
            dst_ref=part,
            send_sem=ring_send.at[q, kind],
            recv_sem=ring_recv.at[q, kind],
            device_id=(e, to),
            device_id_type=MESH,
        )

    def to_right(q):
        return ring(q, 0, x, right)

    def to_left(q):
        return ring(q, 1, x, left)

    def to_other(q):
        return ring(q, 2, x, other)

    def onward(q):
        return ring(q, 3, lx, right) if q % 2 == 0 else ring(q, 3, rx, left)

    def left_to_other(q):
        return ring(q, 4, lx, other)

    def right_to_other(q):
        return ring(q, 5, rx, other)

    def far_to_other(q):
        return ring(q, 6, ox, other)

    def enter(q):
        @pl.loop(1, 16)
        def _(k):
            s1_copy(q, k).wait_recv()

        rows = pl.ds(pl.multiple_of(core * cap, 16), cap)
        gathered[q // 2, x, rows, columns(q)] = matmul_tn(
            pack[...], recv[q // 2, :, columns(q)]
        ).astype(BF16)
        to_right(q).start()
        to_left(q).start()
        to_other(q).start()

    def forward(q):
        to_right(q).wait_recv()
        to_left(q).wait_recv()
        onward(q).start()
        left_to_other(q).start()
        right_to_other(q).start()

    def forward_far(q):
        onward(q).wait_recv()
        far_to_other(q).start()

    slice_d = pl.ds(pl.multiple_of(d * 256, 256), 256)
    my_place = place[:, pl.ds(pl.multiple_of(d * 128, 128), 128)]

    def chip_at(j):
        hop = (j + 1) // 2
        return (x + hop + (j % 2) * (4 - 2 * hop)) % 4

    def project(j):
        chip, slot = chip_at(j), j % 3
        for n in range(TILES):
            gate_up[slot, :, n * 256 : n * 256 + 256] = matmul(
                gathered[0, chip], w[:, n * 256 : n * 256 + 256]
            )

    def finish(j):
        chip, slot = chip_at(j), j % 3
        row = (chip * 2 * cap + iota((2 * cap, 1), 0)).astype(F32)
        gate_row = jnp.concatenate([all_gates[b, 0:1, :] for b in range(8)], axis=1)
        gate = jnp.sum(jnp.where(place[...] == row, gate_row, 0.0), axis=1, keepdims=True)
        dots = jnp.zeros((2 * cap, 128), F32)
        token_rows = gathered[0, chip, :, slice_d].T
        grad_rows = gathered[1, chip, :, slice_d].T

        def upstream(n):
            low = 2 * H + n * 256
            return matmul(gathered[1, chip], w[:, low : min(low + 256, 3 * H)])

        def add_up(rows, low, high):
            acc[:, low:high] += matmul(rows, joint[:, low:high])

        following = upstream(0)
        for n in range(TILES):
            if n % 2 == 0:
                u = following
                if n // 2 + 1 < (TILES + 1) // 2:
                    following = upstream(n // 2 + 1)
            part = u[:, (n % 2) * 128 : (n % 2) * 128 + 128]
            gate_pre = gate_up[slot, :, n * 256 : n * 256 + 128]
            up = gate_up[slot, :, n * 256 + 128 : n * 256 + 256]
            s = 0.5 + 0.5 * jnp.tanh(0.5 * gate_pre)
            active = gate_pre * s
            hidden = active * up
            dots += hidden.astype(BF16).astype(F32) * part
            hidden_grad = gate * part
            joint[:, n * 256 : n * 256 + 128] = (
                hidden_grad * up * (s + active * (1.0 - s))
            ).astype(BF16)
            joint[:, n * 256 + 128 : n * 256 + 256] = (hidden_grad * active).astype(BF16)
            joint[:, 2 * H + n * 128 : 2 * H + n * 128 + 128] = (gate * hidden).astype(BF16)
            if n > 0:
                add_up(token_rows, n * 256 - 256, n * 256)
            if n % 2 == 0 and n > 0:
                add_up(grad_rows, 2 * H + n * 128 - 256, 2 * H + n * 128)
        add_up(token_rows, 2 * H - 256, 2 * H)
        add_up(grad_rows, 3 * H - 128, 3 * H)
        found = my_place == row
        gate_out[...] += jnp.sum(
            jnp.where(found, jnp.sum(dots, axis=1, keepdims=True), 0.0), axis=0, keepdims=True
        )

    back_send, back_recv = send.at[0], recv.at[0]

    def back_copy(k):
        return pltpu.make_async_remote_copy(
            src_ref=block(back_send, peer(k)),
            dst_ref=block(back_recv, e),
            send_sem=back_send_sem.at[k],
            recv_sem=back_recv_sem.at[k],
            device_id=(peer(k), d),
            device_id_type=MESH,
        )

    def send_back():
        own_joint = joint.at[pl.ds(pl.multiple_of(core * cap, 16), cap), :]
        for at in range(0, D, 256):
            own_rows[:, at : at + 256] = matmul_nt(
                own_joint[:, : 2 * H], w[at : at + 256, : 2 * H]
            ).astype(BF16)
        back_send[...] = matmul(pack[...], own_rows[...]).astype(BF16)

        @pl.loop(1, 16)
        def _(k):
            back_copy(k).start()

        back_recv[own, :] = back_send[own, :]

    def combine():
        @pl.loop(1, 16)
        def _(k):
            back_copy(k).wait_recv()

        token_out[...] = matmul_tn(sel[...], back_recv[...]).astype(BF16)

    gate_out[...] = jnp.zeros((1, 128), F32)
    acc[...] = jnp.zeros(acc.shape, F32)
    launch_next(0)
    enter(0)
    launch_next(1)
    enter(1)
    forward(0)

    @pl.loop(1, 8)
    def _(k):
        gate_copy(k).wait_recv()

    @pl.loop(0, TILES)
    def _(n):
        load_part(n, 0).wait()
        load_part(n, 1).wait()

    load_down.wait()
    to_other(0).wait_recv()
    to_other(1).wait_recv()

    @pl.loop(0, 8)
    def _(t):
        @pl.when(t == 1)
        def _():
            launch_next(2)
            enter(2)
            forward(1)
            left_to_other(0).wait_recv()
            left_to_other(1).wait_recv()

        @pl.when(t == 2)
        def _():
            enter(3)
            to_other(2).wait_recv()
            to_other(3).wait_recv()

        @pl.when(t == 3)
        def _():
            forward(2)
            right_to_other(0).wait_recv()
            right_to_other(1).wait_recv()

        @pl.when(t == 4)
        def _():
            forward_far(0)
            forward_far(1)
            send_back()
            forward(3)
            far_to_other(0).wait_recv()
            far_to_other(1).wait_recv()

        @pl.when(t == 5)
        def _():
            left_to_other(2).wait_recv()
            left_to_other(3).wait_recv()

        @pl.when(t == 6)
        def _():
            forward_far(2)
            right_to_other(2).wait_recv()
            right_to_other(3).wait_recv()

        @pl.when(t == 7)
        def _():
            forward_far(3)
            combine()
            far_to_other(2).wait_recv()
            far_to_other(3).wait_recv()

        finishing = (t == 2) | (t >= 5)

        @pl.when(jnp.logical_not(finishing))
        def _():
            project(t - t // 3)

        @pl.when(finishing)
        def _():
            finish((t // 5) * (t - 4))

    for n in range(TILES):
        for part in range(2):
            weight_out[:, part * H + n * 128 : part * H + n * 128 + 128] = acc[
                :, n * 256 + part * 128 : n * 256 + part * 128 + 128
            ].astype(BF16)
    weight_out[:, 2 * H :] = acc[:, 2 * H :].astype(BF16)

    @pl.loop(1, 16)
    def _(k):
        s1_copy(3, k).wait_send()

    for q in range(4):
        for copy in (
            to_right,
            to_left,
            to_other,
            onward,
            left_to_other,
            right_to_other,
            far_to_other,
        ):
            copy(q).wait_send()

    @pl.loop(1, 8)
    def _(k):
        gate_copy(k).wait_send()

    @pl.loop(1, 16)
    def _(k):
        back_copy(k).wait_send()


def layer(cap, picks, gates, tokens, grads, matrix):
    vmem = pl.BlockSpec(memory_space=pltpu.VMEM)
    dma = pltpu.SemaphoreType.DMA
    return pl.pallas_call(
        functools.partial(kernel, cap),
        name=f"moe_backward_{cap}",
        out_shape=(
            pltpu.VMEM((TOK, D), BF16),
            pltpu.VMEM((D // DP, 3 * H), BF16),
            jax.ShapeDtypeStruct((1, ROWS), F32),
            jax.ShapeDtypeStruct((1, 1), F32),
        ),
        in_specs=[vmem, vmem, vmem, vmem, pl.BlockSpec(memory_space=pl.ANY)],
        out_specs=(vmem, vmem, vmem, pl.BlockSpec(memory_space=pltpu.SMEM)),
        scratch_shapes=[
            pltpu.VMEM((D, 3 * H), BF16),
            pltpu.VMEM((2, SLOTS, D), BF16),
            pltpu.VMEM((2, SLOTS, D), BF16),
            pltpu.VMEM((2, 4, 2 * cap, D), BF16),
            pltpu.VMEM((3, 2 * cap, 2 * H), F32),
            pltpu.VMEM((2 * cap, 3 * H), BF16),
            pltpu.VMEM((D // DP, 3 * H), F32),
            pltpu.VMEM((SLOTS, TOK), BF16),
            pltpu.VMEM((SLOTS, cap), BF16),
            pltpu.VMEM((cap, D), BF16),
            pltpu.VMEM((EXPERTS * DP, ROWS), I32),
            pltpu.VMEM((1, 8 * ROWS), F32),
            pltpu.VMEM((8, 8, ROWS), F32),
            dma((2 * TILES + 1,)),
            dma((4, 16)),
            dma((4, 16)),
            dma((8,)),
            dma((8,)),
            dma((4, 7)),
            dma((4, 7)),
            dma((16,)),
            dma((16,)),
        ],
        compiler_params=pltpu.CompilerParams(
            collective_id=0, has_side_effects=True, vmem_limit_bytes=58 * 2**20
        ),
    )(picks, gates, tokens, grads, matrix)


def expert_pass(inputs, upstream, scales, matrix):
    hidden_width = matrix.shape[1] // 3
    gate_up = matrix[:, : 2 * hidden_width]
    down_proj = matrix[:, 2 * hidden_width :]
    projected = jnp.dot(inputs, gate_up, preferred_element_type=jnp.float32)
    gate_pre = projected[:, :hidden_width]
    up_values = projected[:, hidden_width:]
    logistic = jax.nn.sigmoid(gate_pre)
    activated = gate_pre * logistic
    hidden = (activated * up_values).astype(jnp.bfloat16)
    contract = (((1,), (1,)), ((), ()))
    output = lax.dot_general(hidden, down_proj, contract, preferred_element_type=jnp.float32)
    gate_grad = jnp.sum(upstream.astype(jnp.float32) * output, axis=1)
    scaled = (scales[:, None] * upstream.astype(jnp.float32)).astype(jnp.bfloat16)
    hidden_grad = jnp.dot(scaled, down_proj, preferred_element_type=jnp.float32)
    pre_grad = (hidden_grad * up_values * logistic * (1.0 + gate_pre * (1.0 - logistic))).astype(
        jnp.bfloat16
    )
    up_grad = (hidden_grad * activated).astype(jnp.bfloat16)
    joint_grad = jnp.concatenate([pre_grad, up_grad], axis=1)
    token_part = lax.dot_general(joint_grad, gate_up, contract, preferred_element_type=jnp.float32)
    return (token_part, gate_grad, joint_grad, hidden, scaled)


def any_load(tokens, out_grad, weights, gate_values, expert_picks):
    expert_count = lax.axis_size("expert")
    data_count = lax.axis_size("dp")
    holders = expert_count * data_count
    tok_rows = tokens.shape[0]
    width = tokens.shape[1]
    capacity = expert_picks.shape[1]
    rows = capacity // data_count
    slots = 2 * rows // holders
    total_slots = holders * slots
    expert_index = lax.axis_index("expert")
    data_index = lax.axis_index("dp")
    owner_index = expert_index * data_count + data_index
    contract_rows = (((0,), (0,)), ((), ()))
    sources = expert_picks // tok_rows
    held_here = (sources == owner_index).reshape(expert_picks.shape[0], data_count, rows)
    upto = jnp.arange(rows)[:, None] <= jnp.arange(rows)[None, :]
    ranks = matmul(held_here.astype(BF16), upto.astype(BF16)).astype(jnp.int32) - 1
    targets = (
        jnp.arange(expert_picks.shape[0], dtype=jnp.int32)[:, None, None] * data_count
        + jnp.arange(data_count, dtype=jnp.int32)[None, :, None]
    )
    positions = jnp.where(held_here, targets * slots + ranks, total_slots)
    local_rows = (expert_picks - owner_index * tok_rows).reshape(positions.shape)
    slot_table = (
        jnp.full((total_slots,), tok_rows, jnp.int32)
        .at[positions.reshape(-1)]
        .set(local_rows.reshape(-1), mode="drop")
    )
    zero_row = jnp.zeros((1, width), jnp.bfloat16)
    send_tokens = jnp.concatenate([tokens, zero_row], axis=0)[slot_table].reshape(
        holders, slots, width
    )
    send_grads = jnp.concatenate([out_grad, zero_row], axis=0)[slot_table].reshape(
        holders, slots, width
    )
    got_tokens, got_grads = (
        lax.all_to_all(send_tokens, ("expert", "dp"), split_axis=0, concat_axis=0, tiled=True),
        lax.all_to_all(send_grads, ("expert", "dp"), split_axis=0, concat_axis=0, tiled=True),
    )
    flat_tokens = got_tokens.reshape(total_slots, width)
    flat_grads = got_grads.reshape(total_slots, width)
    own_picks = lax.dynamic_slice(expert_picks, (expert_index, data_index * rows), (1, rows))[0]
    pick_sources = own_picks // tok_rows
    steps_index = jnp.arange(rows, dtype=jnp.int32)
    earlier = steps_index[:, None] > steps_index[None, :]
    same_source = pick_sources[:, None] == pick_sources[None, :]
    pick_ranks = jnp.sum((earlier & same_source).astype(jnp.int32), axis=1)
    pick_slots = pick_sources * slots + pick_ranks
    scales = gate_values[0]
    matrix = weights[0]
    inputs = flat_tokens[pick_slots]
    upstream = flat_grads[pick_slots]
    token_part, gate_grad, joint_grad, hidden, scaled = expert_pass(
        inputs, upstream, scales, matrix
    )
    back_rows = jnp.zeros((total_slots, width), jnp.float32).at[pick_slots].set(token_part)
    left_part = lax.dot_general(
        inputs, joint_grad, contract_rows, preferred_element_type=jnp.float32
    )
    right_part = lax.dot_general(scaled, hidden, contract_rows, preferred_element_type=jnp.float32)
    parts = jnp.concatenate([left_part, right_part], axis=1).reshape(data_count, -1, 3 * H)
    summed = jnp.sum(lax.all_to_all(parts, "dp", split_axis=0, concat_axis=0, tiled=True), axis=0)
    weight_grad = summed.astype(jnp.bfloat16)[None]
    returned = lax.all_to_all(
        back_rows.reshape(holders, slots, width),
        ("expert", "dp"),
        split_axis=0,
        concat_axis=0,
        tiled=True,
    )
    token_sum = (
        jnp.zeros((tok_rows + 1, width), jnp.float32)
        .at[slot_table]
        .add(returned.reshape(total_slots, width))
    )
    token_grad = token_sum[:tok_rows].astype(jnp.bfloat16)
    return (token_grad, weight_grad, gate_grad[None])


def copy_kernel(token_in, weight_in, gate_in, token_out, weight_out, gate_out, sems):
    moves = [
        pltpu.make_async_copy(token_in, token_out, sems.at[0]),
        pltpu.make_async_copy(weight_in, weight_out, sems.at[1]),
        pltpu.make_async_copy(gate_in, gate_out, sems.at[2]),
    ]
    for move in moves:
        move.start()
    for move in moves:
        move.wait()


def hand_over(*made):
    return tuple(
        pl.pallas_call(
            copy_kernel,
            name="hand_over",
            out_shape=[jax.ShapeDtypeStruct(m.shape, m.dtype) for m in made],
            in_specs=[pl.BlockSpec(memory_space=pltpu.VMEM)] * 3,
            out_specs=[pl.BlockSpec(memory_space=pl.ANY)] * 3,
            scratch_shapes=[pltpu.SemaphoreType.DMA((3,))],
            compiler_params=pltpu.CompilerParams(vmem_limit_bytes=60 * 2**20),
        )(*made)
    )


CAP = 160


def shards(tokens, out_grad, weights, gate_values, expert_picks):
    *made, most = layer(CAP, expert_picks, gate_values, tokens, out_grad, weights[0])
    given = (tokens, out_grad, weights, gate_values, expert_picks)

    def otherwise(made, given):
        token_grad, weight_grad, gate_grad = any_load(*given)
        return token_grad, weight_grad[0], gate_grad

    token_grad, weight_grad, gate_grad = lax.cond(
        most[0, 0] <= CAP, lambda made, given: hand_over(*made), otherwise, made, given
    )
    return token_grad, weight_grad[None], gate_grad


def solution(mesh):
    return jax.shard_map(
        shards,
        mesh=mesh,
        in_specs=(
            P(("expert", "dp"), None),
            P(("expert", "dp"), None),
            P("expert", None, None),
            P("expert", "dp"),
            P(),
        ),
        out_specs=(P(("expert", "dp"), None), P("expert", "dp", None), P("expert", "dp")),
        check_vma=False,
    )
```
